32 devices in a mesh: grp: 4 (over z), cp: 2 (over x), tp: 4 (over y, core).
Axes of the slice: x: 2, y: 2, z: 4, core: 2. Of those that a mesh axis runs over, the one named last changes fastest.
Arguments:
- inputs: bfloat16 [8, 896, 2048], P('grp', 'cp', 'tp'), may hold values from -6 to 6
- cotangent: bfloat16 [8, 896, 2048], P('grp', 'cp', 'tp'), may hold values from -6 to 6
- attn_gain: bfloat16 [2048], P('cp'), may hold values from 0.25 to 1.75
- query_weight: bfloat16 [2048, 2048], P('cp', 'tp'), may hold values from -0.5 to 0.5
- key_weight: bfloat16 [2048, 512], P('cp', 'tp'), may hold values from -0.5 to 0.5
- value_weight: bfloat16 [2048, 512], P('cp', 'tp'), may hold values from -0.125 to 0.125
- out_weight: bfloat16 [2048, 2048], P('tp', 'cp'), may hold values from -2 to 2
- ffn_gain: bfloat16 [2048], P('cp'), may hold values from 0.25 to 1.75
- gate_weight: bfloat16 [2048, 8192], P('cp', 'tp'), may hold values from -0.125 to 0.125
- up_weight: bfloat16 [2048, 8192], P('cp', 'tp'), may hold values from -0.125 to 0.125
- down_weight: bfloat16 [8192, 2048], P('tp', 'cp'), may hold values from -0.5 to 0.5
- seg_parent: int32 [8, 9], P('grp'), may hold values from 0 to 8, as said below
- seg_start: int32 [8, 9], P('grp'), may hold values from 0 to 832, as said below
- seg_len: int32 [8, 9], P('grp'), may hold values from 64 to 384, as said below
- positions: int32 [8, 896], P('grp'), may hold values from 0 to 511, as said below
Outputs:
- output: bfloat16 [8, 896, 2048], P('grp', 'cp', 'tp')
- input_grad: float32 [8, 896, 2048], P('grp', 'cp', 'tp')
- attn_gain_grad: float32 [2048], P('cp')
- query_grad: float32 [2048, 2048], P('cp', 'tp')
- key_grad: float32 [2048, 512], P('cp', 'tp')
- value_grad: float32 [2048, 512], P('cp', 'tp')
- out_grad: float32 [2048, 2048], P('tp', 'cp')
- ffn_gain_grad: float32 [2048], P('cp')
- gate_grad: float32 [2048, 8192], P('cp', 'tp')
- up_grad: float32 [2048, 8192], P('cp', 'tp')
- down_grad: float32 [8192, 2048], P('tp', 'cp')
The draws below stay inside these ranges and needn't reach their ends.
Inputs may be any that keep to these rules, and one draw needn't show every extreme that they name: `seg_parent`: segments are numbered in the order in which they lie in their tree. One segment is the trunk and is its own parent; four have the trunk as parent; each of the other four has one of those four as parent, and each of those four is the parent of exactly one. The segments of a tree lie end to end in the order of their numbers, starting at token 0, so seg_start is the running sum of seg_len. `seg_len`: every segment has 64 tokens except the trunk, which has 384. The trunk's tokens have positions 0 to 383 in order; a segment whose parent is the trunk starts at 384, the others at 448, rising by one a token.
All inputs are finite; a program needn't handle non-finite values.
Results may differ from the reference program's by a relative error of at most 0.025.
Values may be sent and summed in bfloat16 or wider, within the bound.
No kernel may reach another device: no remote copies, remote signals or barrier semaphores. Data moves between devices by JAX's collectives and lax.ppermute only.
A program may use at most 320 MiB of HBM per device.

```python
import jax
import jax.numpy as jnp
from jax import lax

D = 2048
HQ = 32
HK = 8
HD = 64
FF = 8192
SEG = 64
NSEG = 9
TREE_TOK = 896
TREES = 8


def tree_layout(key):
    base_key = jax.random.fold_in(key, 4099)
    tree_keys = jax.random.split(base_key, TREES)
    role_ids = jnp.arange(NSEG, dtype=jnp.int32)
    role_len = jnp.where(role_ids == 0, 6 * SEG, SEG).astype(jnp.int32)
    role_depth = jnp.where(role_ids == 0, 0, jnp.where(role_ids < 5, 6 * SEG, 7 * SEG)).astype(jnp.int32)
    tokens = jnp.arange(TREE_TOK, dtype=jnp.int32)

    def one_tree(tree_key):
        key_order, key_leaf = jax.random.split(tree_key)
        packing = jax.random.permutation(key_order, NSEG).astype(jnp.int32)
        pairing = jax.random.permutation(key_leaf, 4).astype(jnp.int32)
        role_parent = jnp.concatenate([jnp.zeros((5,), jnp.int32), pairing + 1])
        slot_of = jnp.zeros((NSEG,), jnp.int32).at[packing].set(role_ids)
        lengths = role_len[packing]
        starts = jnp.cumsum(lengths) - lengths
        parents = slot_of[role_parent[packing]]
        segment_of = jnp.sum((tokens[:, None] >= starts[None, :]).astype(jnp.int32), axis=1) - 1
        path_depth = role_depth[packing][segment_of] + tokens - starts[segment_of]
        return (parents, starts, lengths, path_depth)
    return jax.vmap(one_tree)(tree_keys)


def draw_seg_parent(key, part):
    return tree_layout(key)[0]


def draw_seg_start(key, part):
    return tree_layout(key)[1]


def draw_seg_len(key, part):
    return tree_layout(key)[2]


def draw_positions(key, part):
    return tree_layout(key)[3]


def steps_of(stream_key, dims, cuts, smallest, top_value):
    level = 1.0
    for dim, blocks in cuts:
        heights = jax.random.uniform(jax.random.fold_in(jax.random.fold_in(stream_key, 6), dim), (blocks,), jnp.float32, smallest / len(cuts), top_value / len(cuts))
        level = level * jnp.repeat(jnp.exp(heights), dims[dim] // blocks).reshape((-1,) + (1,) * (len(dims) - 1 - dim))
    return level


def normal_values(key, dims, scale, limit, cuts=(), kind=jnp.bfloat16):
    gain = steps_of(key, dims, cuts, -0.22, 0.18) if cuts else 1.0
    array = jax.random.normal(key, dims, jnp.float32) * scale * gain
    return jnp.minimum(jnp.maximum(array, -limit), limit).astype(kind)


def setup_inputs(seed: int = 0) -> dict:
    splits = jax.random.split(jax.random.key(seed), 16)
    inputs = normal_values(splits[0], (TREES, TREE_TOK, D), 1.0, 6.0, ((0, 4), (1, 2), (2, 4)))
    cotangent = normal_values(splits[1], (TREES, TREE_TOK, D), 1.0, 6.0, ((0, 4), (1, 2), (2, 4)))
    attn_gain = jnp.clip(1.0 + 0.15 * jax.random.normal(splits[2], (D,), jnp.float32), 0.25, 1.75).astype(jnp.bfloat16)
    query_weight = normal_values(splits[3], (D, HQ * HD), (D // 16) ** -0.5, 0.5, ((0, 2), (1, 4)))
    key_weight = normal_values(splits[4], (D, HK * HD), (D // 16) ** -0.5, 0.5, ((0, 2), (1, 4)))
    value_weight = normal_values(splits[5], (D, HK * HD), D ** -0.5, 0.125, ((0, 2), (1, 4)))
    out_weight = normal_values(splits[6], (HQ * HD, D), (HD // 8) ** -0.5, 2.0, ((0, 4), (1, 2)))
    ffn_gain = jnp.clip(1.0 + 0.15 * jax.random.normal(splits[7], (D,), jnp.float32), 0.25, 1.75).astype(jnp.bfloat16)
    gate_weight = normal_values(splits[8], (D, FF), D ** -0.5, 0.125, ((0, 2), (1, 4)))
    up_weight = normal_values(splits[9], (D, FF), D ** -0.5, 0.125, ((0, 2), (1, 4)))
    down_weight = normal_values(splits[10], (FF, D), (FF // 64) ** -0.5, 0.5, ((0, 4), (1, 2)))
    seg_parent = draw_seg_parent(jax.random.fold_in(splits[15], 71), 0)
    seg_start = draw_seg_start(jax.random.fold_in(splits[15], 71), 0)
    seg_len = draw_seg_len(jax.random.fold_in(splits[15], 71), 0)
    positions = draw_positions(jax.random.fold_in(splits[15], 71), 0)
    return {"inputs": inputs, "cotangent": cotangent, "attn_gain": attn_gain, "query_weight": query_weight, "key_weight": key_weight, "value_weight": value_weight, "out_weight": out_weight, "ffn_gain": ffn_gain, "gate_weight": gate_weight, "up_weight": up_weight, "down_weight": down_weight, "seg_parent": seg_parent, "seg_start": seg_start, "seg_len": seg_len, "positions": positions}


norm_eps = 1e-05
att_scale = 0.015625
resid_scale = 0.22
rope_base = 10000000.0
highest = lax.Precision.HIGHEST

@jax.custom_vjp
def low(v):
    return lax.optimization_barrier(v.astype(jnp.bfloat16)).astype(jnp.float32)

@jax.custom_vjp
def low_back(v):
    return v

def low_keep(v):
    return (low(v), None)

def low_pass(kept, grad):
    return (grad,)

def back_keep(v):
    return (v, None)

def back_low(kept, grad):
    return (low(grad),)
low.defvjp(low_keep, low_pass)
low_back.defvjp(back_keep, back_low)

def rope_tables(position):
    half_dim = HD // 2
    freq_index = jnp.arange(half_dim, dtype=jnp.float32)
    inverse = jnp.power(jnp.float32(rope_base), freq_index * (-2.0 / HD))
    angles = position.astype(jnp.float32)[..., None] * inverse
    cosine_table = jnp.concatenate([jnp.cos(angles), jnp.cos(angles)], axis=-1)[..., None, :]
    sine_table = jnp.concatenate([jnp.sin(angles), jnp.sin(angles)], axis=-1)[..., None, :]
    return (cosine_table, sine_table)

def rotate(values, cosine_table, sine_table):
    half_dim = values.shape[-1] // 2
    turned = jnp.concatenate([-values[..., half_dim:], values[..., :half_dim]], axis=-1)
    return values * cosine_table + turned * sine_table

def tree_allowed(parents, starts, lengths, position):
    tok_count = position.shape[0]
    token_ids = jnp.arange(tok_count, dtype=jnp.int32)
    slot_ids = jnp.arange(parents.shape[0], dtype=jnp.int32)
    member = (token_ids[:, None] >= starts[None, :]) & (token_ids[:, None] < (starts + lengths)[None, :])
    seg_of = lax.optimization_barrier(jnp.sum(jnp.where(member, slot_ids[None, :], 0), axis=1)).astype(jnp.int32)
    parent_of = parents[seg_of].astype(jnp.int32)
    grand_of = parents[parent_of].astype(jnp.int32)
    key_seg = seg_of[None, :]
    linked = (key_seg == seg_of[:, None]) | (key_seg == parent_of[:, None]) | (key_seg == grand_of[:, None])
    return linked & (position[None, :] <= position[:, None])

def attend_block(queries, allowed, key_rows, value_rows):
    row_count = queries.shape[0]
    grouped = queries.reshape(row_count, HK, HQ // HK, HD)
    scores = jnp.einsum('rhgd,nhd->hgrn', grouped, key_rows, precision=highest) * att_scale
    scores = low_back(scores)
    scores = jnp.where(allowed[None, None], scores, -1e+30)
    row_top = lax.optimization_barrier(jnp.max(scores, axis=-1, keepdims=True))
    powered = jnp.exp(scores - row_top)
    weights = low(powered / lax.optimization_barrier(jnp.sum(powered, axis=-1, keepdims=True)))
    mixture = jnp.einsum('hgrn,nhd->rhgd', weights, value_rows, precision=highest)
    return mixture.reshape(row_count, HQ * HD)

def block_forward(inputs, attn_gain, query_weight, key_weight, value_weight, out_weight, ffn_gain, gate_weight, up_weight, down_weight, cosine_table, sine_table, allowed):
    tok_count = inputs.shape[0]
    scale_attn = lax.rsqrt(lax.optimization_barrier(jnp.mean(inputs * inputs, axis=-1, keepdims=True)) + norm_eps)
    normed = low(inputs * scale_attn * attn_gain)
    queries = low_back(jnp.dot(normed, query_weight, precision=highest)).reshape(tok_count, HQ, HD)
    key_rows = low_back(jnp.dot(normed, key_weight, precision=highest)).reshape(tok_count, HK, HD)
    value_rows = low(low_back(jnp.dot(normed, value_weight, precision=highest))).reshape(tok_count, HK, HD)
    queries = low(rotate(queries, cosine_table, sine_table))
    key_rows = low(rotate(key_rows, cosine_table, sine_table))
    blocks = 7
    checked = jax.checkpoint(attend_block)
    mixture = lax.map(lambda block_pair: checked(block_pair[0], block_pair[1], key_rows, value_rows), (queries.reshape(blocks, tok_count // blocks, HQ, HD), allowed.reshape(blocks, tok_count // blocks, tok_count)))
    mixture = low_back(low(mixture.reshape(tok_count, HQ * HD)))
    attn_out = low_back(jnp.dot(mixture, out_weight, precision=highest))
    hidden = inputs + resid_scale * attn_out
    scale_ffn = lax.rsqrt(lax.optimization_barrier(jnp.mean(hidden * hidden, axis=-1, keepdims=True)) + norm_eps)
    normed_ffn = low(hidden * scale_ffn * ffn_gain)
    gate_pre = low_back(jnp.dot(normed_ffn, gate_weight, precision=highest))
    up_proj = low_back(jnp.dot(normed_ffn, up_weight, precision=highest))
    activation = low(gate_pre * jax.nn.sigmoid(gate_pre) * up_proj)
    ffn_out = low_back(jnp.dot(activation, down_weight, precision=highest))
    return hidden + resid_scale * ffn_out

def reference(inputs, cotangent, attn_gain, query_weight, key_weight, value_weight, out_weight, ffn_gain, gate_weight, up_weight, down_weight, seg_parent, seg_start, seg_len, positions):
    params = tuple((weight_arr.astype(jnp.float32) for weight_arr in (attn_gain, query_weight, key_weight, value_weight, out_weight, ffn_gain, gate_weight, up_weight, down_weight)))

    def per_tree(running, tree_data):
        tree_in, tree_cot, parents, starts, lengths, position = tree_data
        cosine_table, sine_table = rope_tables(position)
        allowed = tree_allowed(parents, starts, lengths, position)

        def forward(tree_x, *weight_set):
            return block_forward(tree_x, *weight_set, cosine_table, sine_table, allowed)
        result, pullback = jax.vjp(forward, tree_in.astype(jnp.float32), *params)
        gradients = pullback(tree_cot.astype(jnp.float32))
        running = tuple((summed + grad_part for summed, grad_part in zip(running, gradients[1:])))
        return (running, (result.astype(jnp.bfloat16), gradients[0]))
    zeros_init = tuple((jnp.zeros(weight_arr.shape, jnp.float32) for weight_arr in params))
    totals, (outputs, input_grads) = lax.scan(per_tree, zeros_init, (inputs, cotangent, seg_parent, seg_start, seg_len, positions))
    return (outputs, input_grads, totals[0], totals[1], totals[2], totals[3], totals[4], totals[5], totals[6], totals[7], totals[8])
```

```python
import functools
import math

import jax
import jax.numpy as jnp
from jax import lax
from jax.experimental import pallas as pl
from jax.experimental.pallas import tpu as pltpu
from jax.sharding import PartitionSpec as P

HD = 64

norm_eps = 1e-05
att_scale = 0.015625
resid_scale = 0.22
rope_base = 10000000.0
masked_score = -1e30

low = jnp.bfloat16
wide = jnp.float32


def tie(value, *earlier):
    return lax.optimization_barrier((value,) + earlier)[0] if earlier else value


class Lane:
    def __init__(self, depth):
        self.depth = depth
        self.done = []

    def move(self, block, axis, pairs, *earlier):
        if len(self.done) >= self.depth:
            earlier = (self.done[-self.depth],) + earlier
        self.done.append(lax.ppermute(tie(block, *earlier), axis, pairs))
        return self.done[-1]


class Clock:
    def __init__(self):
        self.last = ()

    def run(self, function, *given):
        given = lax.optimization_barrier(given + self.last)[: len(given)]
        result = function(*given)
        self.last = (jax.tree.leaves(result)[0],)
        return result


def cp_fetch(lane, block):
    count = lax.axis_size("cp")
    return [
        lane.move(block, "cp", [((i + s) % count, i) for i in range(count)])
        for s in range(1, count)
    ]


def cp_deliver(lane, block, shift):
    count = lax.axis_size("cp")
    return lane.move(block, "cp", [(i, (i + shift) % count) for i in range(count)])


def in_order(flag, first, second):
    return [jnp.where(flag, first, second), jnp.where(flag, second, first)]


class LineGather:
    def __init__(self, lane, block, *earlier):
        self.lane, self.block = lane, block
        self.near = lane.move(block, "grp", [(0, 1), (1, 0), (2, 3), (3, 2)], *earlier)
        self.pair = jnp.concatenate(in_order(lax.axis_index("grp") % 2 == 0, block, self.near), axis=0)

    def across(self, *earlier):
        self.far = self.lane.move(self.pair, "grp", [(1, 2), (2, 1)], *earlier)

    def out(self, *earlier):
        self.passed = self.lane.move(self.far, "grp", [(1, 0), (2, 3)], *earlier)


def assemble_kernel(here_ref, own_ref, *refs, own_blocks, straight_blocks, share_blocks, beside):
    step, here = pl.program_id(0), here_ref[0]
    straight = refs[:1] if straight_blocks else ()
    share_ref, near_ref, far_ref, passed_ref, out_ref = refs[len(straight) :]
    width = own_ref.shape[1]
    at = step if beside else step - own_blocks
    target = out_ref.at[:, width:] if beside else out_ref
    if beside:
        out_ref[:, :width] = own_ref[...]
    else:

        @pl.when(at < 0)
        def _():
            target[...] = own_ref[...]

    if straight:

        @pl.when((at >= 0) & (at < straight_blocks))
        def _():
            target[...] = straight[0][...]

    place = at - straight_blocks
    owner = lax.div(jnp.maximum(place, 0), share_blocks)
    there = place >= 0
    near = owner == here + 1 - 2 * lax.rem(here, 2)
    apart = lax.div(owner, 2) != lax.div(here, 2)
    inner = (here == 1) | (here == 2)

    @pl.when(there & (owner == here))
    def _():
        target[...] = share_ref[...]

    @pl.when(there & near)
    def _():
        target[...] = near_ref[...]

    @pl.when(there & apart & inner)
    def _():
        target[...] = far_ref[...]

    @pl.when(there & apart & jnp.logical_not(inner))
    def _():
        target[...] = passed_ref[...]


def assemble_shared(weight, straight, line, beside):
    share = line.block.shape[0]
    rows, width = weight.shape
    direct = straight[0].shape[0] if straight else 0
    unit = math.gcd(math.gcd(rows, direct), share)
    own_blocks, straight_blocks, share_blocks = rows // unit, direct // unit, share // unit
    offset = straight_blocks + (0 if beside else own_blocks)
    spec = lambda first, count: pl.BlockSpec(
        (unit, width), lambda i, here: (jnp.clip(i - first(here[0]), 0, count - 1), 0)
    )
    own_spec = spec(lambda z: 0, own_blocks)
    straight_spec = [spec(lambda z: offset - straight_blocks, straight_blocks)] if direct else []
    pair_first = lambda z: offset + (2 - 2 * lax.div(z, 2)) * share_blocks
    specs = [own_spec] + straight_spec + [
        spec(lambda z: offset + z * share_blocks, share_blocks),
        spec(lambda z: offset + (z + 1 - 2 * lax.rem(z, 2)) * share_blocks, share_blocks),
        spec(pair_first, 2 * share_blocks),
        spec(pair_first, 2 * share_blocks),
    ]
    out_shape = (rows, 2 * width) if beside else (2 * rows, width)
    return pl.pallas_call(
        functools.partial(
            assemble_kernel,
            own_blocks=own_blocks,
            straight_blocks=straight_blocks,
            share_blocks=share_blocks,
            beside=beside,
        ),
        grid_spec=pltpu.PrefetchScalarGridSpec(
            num_scalar_prefetch=1,
            grid=(out_shape[0] // unit,),
            in_specs=specs,
            out_specs=pl.BlockSpec((unit, out_shape[1]), lambda i, here: (i, 0)),
        ),
        out_shape=jax.ShapeDtypeStruct(out_shape, weight.dtype),
        cost_estimate=pl.CostEstimate(
            flops=0, bytes_accessed=8 * rows * width + 2 * share * width, transcendentals=0
        ),
        name="assemble",
    )(
        lax.axis_index("grp").astype(jnp.int32).reshape(1),
        weight,
        *straight,
        line.block,
        line.near,
        line.far,
        line.passed,
    )


class LineSum:
    lag = 3

    def __init__(self, clock):
        here = lax.axis_index("grp")
        self.inner = (here == 1) | (here == 2)
        self.clock = clock
        self.parts, self.sums, self.totals = [], [], []
        self.ins, self.acrosses, self.outs, self.loads = [], [], [], []

    def load(self, part):
        self.parts.append(part)
        back = len(self.parts) - 1 - self.lag
        total = self.totals[back] if back >= 0 else None
        if part is None or total is None or part.shape[1] != total.shape[1]:
            self.loads.append((part, total))
            return
        height = max(part.shape[0], total.shape[0])

        def choose(part, total):
            fill = lambda v: jnp.pad(v, ((0, height - v.shape[0]), (0, 0)))
            return jnp.where(self.inner, fill(total), fill(part))

        self.loads.append(self.clock.run(choose, part, total))

    def step(self):
        count = len(self.loads) - 1
        before = self.ins[-1:] + self.outs[-1:]
        load = self.loads[count]
        if isinstance(load, tuple):
            part, total = load
            if part is not None:
                self.ins.append(lax.ppermute(tie(part, *before), "grp", [(0, 1), (3, 2)]))
            if total is not None:
                self.outs.append(lax.ppermute(tie(total, *before), "grp", [(1, 0), (2, 3)]))
        else:
            side = lax.ppermute(tie(load, *before), "grp", [(0, 1), (1, 0), (2, 3), (3, 2)])
            self.ins.append(side)
            self.outs.append(side)
        if count >= 1 and self.parts[count - 1] is not None:
            part, got = self.parts[count - 1], self.ins[count - 1]
            total = self.clock.run(lambda p, g: p + g[: p.shape[0]], part, got)
            self.sums.append(total)
            self.acrosses.append(
                lax.ppermute(tie(total, *self.acrosses[-1:]), "grp", [(1, 2), (2, 1)])
            )
        if count >= 2 and self.parts[count - 2] is not None:
            self.totals.append(
                self.clock.run(lambda a, b: a + b, self.sums[count - 2], self.acrosses[count - 2])
            )

    def final(self, index):
        total, got = self.totals[index], self.outs[index]
        return jnp.where(self.inner, total, got[: total.shape[0]]).astype(wide)


def tp_swap(block, bit, *earlier):
    count = lax.axis_size("tp")
    return lax.ppermute(tie(block, *earlier), "tp", [(i, i ^ bit) for i in range(count)])


class TpTotal:
    def __init__(self, part):
        self.plain = None
        if lax.axis_size("tp") != 4:
            self.plain = lax.psum(part.astype(low), "tp")
            return
        half = part.shape[0] // 2
        self.odd = lax.axis_index("tp") % 2
        self.mine = lax.dynamic_slice_in_dim(part, self.odd * half, half, 0)
        theirs = lax.dynamic_slice_in_dim(part, (1 - self.odd) * half, half, 0)
        self.got = tp_swap(theirs.astype(low), 1)

    def across(self, *earlier):
        if self.plain is None:
            self.pair = (self.mine.astype(wide) + self.got.astype(wide)).astype(low)
            self.far = tp_swap(self.pair, 2, *earlier)
            return self.far
        return self.plain

    def back(self, *earlier):
        if self.plain is None:
            self.total = (self.pair.astype(wide) + self.far.astype(wide)).astype(low)
            self.other = tp_swap(self.total, 1, *earlier)
            return self.other
        return self.plain

    def value(self):
        if self.plain is None:
            return jnp.concatenate(in_order(self.odd == 0, self.total, self.other), axis=0)
        return self.plain


def attend_kernel(
    q_ref, k_ref, v_ref, row_ref, col_ref, o_ref, lse_ref, bias_ref, *, per_kv
):
    step = pl.program_id(0)
    group = (2 * step) // per_kv

    @pl.when(step == 0)
    def _():
        seg, par, grand, pos = (row_ref[:, i : i + 1] for i in range(4))
        key_seg, key_pos = col_ref[0:1, :], col_ref[1:2, :]
        linked = (key_seg == seg) | (key_seg == par) | (key_seg == grand)
        bias_ref[...] = jnp.where(linked & (key_pos <= pos), 0.0, masked_score)

    k = jnp.where(group == 0, k_ref[:, :HD], k_ref[:, HD : 2 * HD])
    v = jnp.where(group == 0, v_ref[:, :HD], v_ref[:, HD : 2 * HD])
    outs, totals = [], []
    for h in range(2):
        q = q_ref[:, h * HD : (h + 1) * HD]
        s = lax.dot_general(q, k, (((1,), (1,)), ((), ())), preferred_element_type=wide)
        s = s + bias_ref[...]
        top = jnp.max(s, axis=-1, keepdims=True)
        p = jnp.exp(s - top)
        norm = jnp.sum(p, axis=-1, keepdims=True)
        o = jnp.dot(p.astype(low), v, preferred_element_type=wide)
        outs.append(o / norm)
        totals.append(top + jnp.log(norm))
    o_ref[...] = jnp.concatenate(outs, axis=1).astype(low)
    lse_ref[...] = jnp.concatenate([jnp.broadcast_to(t, (t.shape[0], HD)) for t in totals], axis=1)


def attend(q, k, v, row_meta, col_meta, per_kv):
    rows, width = q.shape
    keys, kv_width = k.shape
    pairs = width // (2 * HD)
    whole = lambda a: pl.BlockSpec(a.shape, lambda j: (0, 0))
    tile = pl.BlockSpec((rows, 2 * HD), lambda j: (0, j))
    heads = 2 * pairs
    return pl.pallas_call(
        functools.partial(attend_kernel, per_kv=per_kv),
        grid=(pairs,),
        in_specs=[tile, whole(k), whole(v), whole(row_meta), whole(col_meta)],
        out_specs=[tile, tile],
        out_shape=[
            jax.ShapeDtypeStruct((rows, width), low),
            jax.ShapeDtypeStruct((rows, width), wide),
        ],
        scratch_shapes=[pltpu.VMEM((rows, keys), wide)],
        cost_estimate=pl.CostEstimate(
            flops=16 * heads * rows * keys * HD,
            bytes_accessed=8 * rows * width + 4 * keys * kv_width,
            transcendentals=heads * rows * keys,
        ),
        name="attend",
    )(q, k, v, row_meta, col_meta)


def attend_back_kernel(
    q_ref, k_ref, v_ref, g_ref, lse_ref, row_ref, col_ref, dq_ref, dk_ref, dv_ref, bias_ref, dk_sum, dv_sum, *, per_kv
):
    step = pl.program_id(0)
    group = (2 * step) // per_kv
    pairs_kv = per_kv // 2

    @pl.when(step == 0)
    def _():
        seg, par, grand, pos = (row_ref[i : i + 1, :] for i in range(4))
        key_seg, key_pos = col_ref[:, 0:1], col_ref[:, 1:2]
        linked = (key_seg == seg) | (key_seg == par) | (key_seg == grand)
        bias_ref[...] = jnp.where(linked & (key_pos <= pos), 0.0, masked_score)

    k = jnp.where(group == 0, k_ref[:, :HD], k_ref[:, HD : 2 * HD])
    v = jnp.where(group == 0, v_ref[:, :HD], v_ref[:, HD : 2 * HD])
    outs = []
    dk = jnp.zeros(k.shape, wide)
    dv = jnp.zeros(k.shape, wide)
    nt = (((1,), (1,)), ((), ()))
    for h in range(2):
        q = q_ref[:, h * HD : (h + 1) * HD]
        g = g_ref[:, h * HD : (h + 1) * HD]
        s = lax.dot_general(k, q, nt, preferred_element_type=wide) + bias_ref[...]
        p = jnp.exp(s - lse_ref[0, h : h + 1, :])
        dp = lax.dot_general(v, g, nt, preferred_element_type=wide)
        dv = dv + jnp.dot(p.astype(low), g, preferred_element_type=wide)
        mean = jnp.sum(p * dp, axis=0, keepdims=True)
        dz = (p * (dp - mean)).astype(low)
        dk = dk + jnp.dot(dz, q, preferred_element_type=wide)
        dq = lax.dot_general(dz, k, (((0,), (0,)), ((), ())), preferred_element_type=wide)
        outs.append(dq * att_scale)
    dq_ref[...] = jnp.concatenate(outs, axis=1)
    first = lax.rem(step, pairs_kv) == 0

    @pl.when(first)
    def _():
        dk_sum[...] = dk
        dv_sum[...] = dv

    @pl.when(jnp.logical_not(first))
    def _():
        dk_sum[...] += dk
        dv_sum[...] += dv

    for which in range(2):

        @pl.when(step == (which + 1) * pairs_kv - 1)
        def _():
            dk_ref[:, which * HD : (which + 1) * HD] = dk_sum[...]
            dv_ref[:, which * HD : (which + 1) * HD] = dv_sum[...]


def attend_back(q, k, v, g, lse, row_meta, col_meta, per_kv):
    rows, width = q.shape
    keys, kv_width = k.shape
    pairs = width // (2 * HD)
    heads = 2 * pairs
    whole = lambda a: pl.BlockSpec(a.shape, lambda j: (0, 0))
    tile = pl.BlockSpec((rows, 2 * HD), lambda j: (0, j))
    return pl.pallas_call(
        functools.partial(attend_back_kernel, per_kv=per_kv),
        grid=(pairs,),
        in_specs=[
            tile,
            whole(k),
            whole(v),
            tile,
            pl.BlockSpec((1, 2, rows), lambda j: (j, 0, 0)),
            whole(row_meta),
            whole(col_meta),
        ],
        out_specs=[tile, whole(k), whole(v)],
        out_shape=[
            jax.ShapeDtypeStruct((rows, width), wide),
            jax.ShapeDtypeStruct((keys, kv_width), wide),
            jax.ShapeDtypeStruct((keys, kv_width), wide),
        ],
        scratch_shapes=[
            pltpu.VMEM((keys, rows), wide),
            pltpu.VMEM((keys, HD), wide),
            pltpu.VMEM((keys, HD), wide),
        ],
        cost_estimate=pl.CostEstimate(
            flops=40 * heads * rows * keys * HD,
            bytes_accessed=8 * rows * width + 12 * keys * kv_width,
            transcendentals=heads * rows * keys,
        ),
        name="attend_back",
    )(q, k, v, g, lse, row_meta, col_meta)


def rope_tables(position, repeats):
    half_dim = HD // 2
    freq_index = jnp.arange(half_dim, dtype=wide)
    inverse = jnp.power(wide(rope_base), freq_index * (-2.0 / HD))
    angles = position.astype(wide)[:, None] * inverse
    tile = lambda table: jnp.tile(table, (1, 2 * repeats))
    return tile(jnp.cos(angles)), tile(jnp.sin(angles))


def turn(values):
    half_dim = HD // 2
    front = lax.broadcasted_iota(jnp.int32, values.shape, 1) % HD < half_dim
    return jnp.where(
        front, -jnp.roll(values, -half_dim, axis=1), jnp.roll(values, half_dim, axis=1)
    )


def norm_back(norm_grad, normed_unit, inv_scale, gain_vec):
    scaled = norm_grad * gain_vec
    return inv_scale * (
        scaled - normed_unit * jnp.mean(scaled * normed_unit, axis=-1, keepdims=True)
    )


def matmul(a, b):
    return jnp.dot(a, b, preferred_element_type=wide)


def matmul_nt(a, b):
    return lax.dot_general(a, b, (((1,), (1,)), ((), ())), preferred_element_type=wide)


def matmul_tn(a, b):
    return lax.dot_general(a, b, (((0,), (0,)), ((), ())), preferred_element_type=wide)


def tree_segments(seg_parent, seg_start, seg_len, key_count):
    token_ids = jnp.arange(key_count, dtype=jnp.int32)
    slot_ids = jnp.arange(seg_parent.shape[1], dtype=jnp.int32)
    member = (token_ids[None, :, None] >= seg_start[:, None, :]) & (
        token_ids[None, :, None] < (seg_start + seg_len)[:, None, :]
    )
    pick = lambda table: jnp.sum(jnp.where(member, table[:, None, :], 0), axis=2)
    grand_parent = jnp.sum(
        jnp.where(seg_parent[:, :, None] == slot_ids[None, None, :], seg_parent[:, None, :], 0),
        axis=2,
    )
    return (
        pick(jnp.broadcast_to(slot_ids[None, :], seg_parent.shape)),
        pick(seg_parent),
        pick(grand_parent),
    )


def per_device(
    inputs,
    cotangent,
    attn_gain,
    query_weight,
    key_weight,
    value_weight,
    out_weight,
    ffn_gain,
    gate_weight,
    up_weight,
    down_weight,
    seg_parent,
    seg_start,
    seg_len,
    positions,
):
    trees, rows, part_width = inputs.shape
    keys = positions.shape[1]
    block = attn_gain.shape[0]
    cp_count, tp_count, grp_count = lax.axis_size("cp"), lax.axis_size("tp"), lax.axis_size("grp")
    model_width = block * cp_count
    q_width, kv_width = query_weight.shape[1], key_weight.shape[1]
    per_kv = q_width // kv_width
    tokens = trees * rows
    cp_here, tp_here = lax.axis_index("cp"), lax.axis_index("tp")

    def rolled(values):
        return lax.dynamic_slice_in_dim(
            jnp.concatenate([values, values], axis=-1), cp_here * block, model_width, values.ndim - 1
        )

    def width_part(values, owner):
        start = (owner * part_width - cp_here * block) % model_width
        if block % part_width:
            values = jnp.concatenate([values, values], axis=-1)
        return lax.dynamic_slice_in_dim(values, start, part_width, 1)

    def tp_width(shard, *earlier):
        shard = tie(shard.reshape(tokens, part_width), *earlier)
        if tp_count != 4:
            return rolled(lax.all_gather(shard, "tp", axis=1, tiled=True)), shard
        far = tp_swap(shard, 2)
        near = tp_swap(jnp.stack([shard, far]), 1)
        pieces = [shard, near[0], far, near[1]]
        picks = [lax.select_n(tp_here, *[pieces[j ^ m] for m in range(4)]) for j in range(4)]
        return rolled(jnp.concatenate(picks, axis=1)), far

    def tp_scatter(part):
        if tp_count != 4:
            natural = lax.dynamic_slice_in_dim(
                jnp.concatenate([part, part], axis=-1),
                (model_width - cp_here * block) % model_width,
                model_width,
                1,
            )
            return lax.psum_scatter(
                natural.astype(low), "tp", scatter_dimension=1, tiled=True
            ).astype(wide)
        sent = jnp.concatenate([width_part(part, tp_here ^ 1), width_part(part, tp_here ^ 3)], axis=1)
        got = tp_swap(sent.astype(low), 1).astype(wide)
        kept = width_part(part, tp_here) + got[:, :part_width]
        passed = width_part(part, tp_here ^ 2) + got[:, part_width:]
        return kept + tp_swap(passed.astype(low), 2).astype(wide)

    lane, line = Lane(2), Lane(2)
    shared = cp_count == 2 and grp_count == 4

    def share_of(weight, direct):
        if not shared:
            return None
        share = (weight.shape[0] - direct) // grp_count
        start = direct + lax.axis_index("grp") * share
        return cp_fetch(lane, lax.dynamic_slice_in_dim(weight, start, share, 0))[0]

    def direct_of(weight, direct):
        if not shared:
            return cp_fetch(lane, weight)
        return cp_fetch(lane, weight[:direct]) if direct else []

    def assemble(weight, straight, gathered, beside):
        if shared:
            return assemble_shared(weight, straight, gathered, beside)
        return jnp.concatenate([weight] + straight, axis=1 if beside else 0)

    qkv_own = jnp.concatenate([query_weight, key_weight, value_weight], axis=1)
    gains_own = jnp.stack([attn_gain, ffn_gain])
    up_direct, down_direct = up_weight.shape[0] // 2, down_weight.shape[0] // 4
    input_rows, input_far = tp_width(inputs)
    gains = jnp.concatenate([gains_own] + cp_fetch(lane, gains_own), axis=1).astype(wide)
    attn_gain_full, ffn_gain_full = gains[0:1], gains[1:2]
    gate_share = share_of(gate_weight, 0)
    qkv_full = jnp.concatenate([qkv_own] + cp_fetch(lane, qkv_own), axis=0)
    up_share = share_of(up_weight, up_direct)
    gate_line = LineGather(line, gate_share) if shared else None
    cot_rows, _ = tp_width(cotangent, input_rows)

    seg, parent, grand = tree_segments(seg_parent, seg_start, seg_len, keys)
    meta = jnp.stack([seg, parent, grand, positions], axis=1)
    first_row = cp_here * rows
    row_meta_t = lax.dynamic_slice_in_dim(meta, first_row, rows, 2)
    key_meta = lax.dynamic_slice_in_dim(
        jnp.concatenate([meta[:, 0::3], meta[:, 0::3]], axis=2), first_row, keys, 2
    )
    row_meta = jnp.swapaxes(row_meta_t, 1, 2)
    key_meta_t = jnp.swapaxes(key_meta, 1, 2)
    own_pos = row_meta_t[:, 3].reshape(tokens)
    cos_qk, sin_qk = rope_tables(own_pos, (q_width + kv_width) // HD)

    input_wide = input_rows.astype(wide)
    scale_attn = lax.rsqrt(jnp.mean(input_wide * input_wide, axis=-1, keepdims=True) + norm_eps)
    unit_attn = input_wide * scale_attn
    normed_attn = (unit_attn * attn_gain_full).astype(low)
    qkv_raw = matmul(normed_attn, qkv_full)
    qk_raw = qkv_raw[:, : q_width + kv_width]
    qk_rot = qk_raw * cos_qk + turn(qk_raw) * sin_qk
    query_low = qk_rot[:, :q_width].astype(low) * low(att_scale)
    key_low = qk_rot[:, q_width:].astype(low)
    kv_own = jnp.concatenate([key_low, qkv_raw[:, q_width + kv_width :].astype(low)], axis=1)
    kv_sets = [
        jnp.concatenate([own] + cp_fetch(lane, own), axis=0)
        for own in (kv_own[t * rows : (t + 1) * rows] for t in range(trees))
    ]
    out_full = jnp.concatenate([out_weight] + cp_fetch(lane, out_weight), axis=1)
    up_straight = direct_of(up_weight, up_direct)
    down_share = share_of(down_weight, down_direct)
    down_straight = direct_of(down_weight, down_direct)
    gate_straight = [] if shared else direct_of(gate_weight, 0)
    clock = Clock()
    up_line = down_line = None
    if shared:
        gate_line.across(query_low)
        up_line = LineGather(line, up_share, query_low)
    mixtures, lses, sums = [], [], []
    for tree in range(trees):
        here = slice(tree * rows, (tree + 1) * rows)
        mixture, lse = clock.run(
            lambda q, kv: attend(
                q, kv[:, :kv_width], kv[:, kv_width:], row_meta[tree], key_meta[tree], per_kv
            ),
            query_low[here],
            kv_sets[tree],
        )
        mixtures.append(mixture)
        lses.append(lse)
        sums.append(TpTotal(clock.run(matmul, mixture, out_full)))
    mixture_all = jnp.concatenate(mixtures, axis=0)
    for one in sums:
        one.across()
    if shared:
        gate_line.out(sums[-1].pair)
        up_line.across(sums[-1].pair)
        up_line.out()
        down_line = LineGather(line, down_share, sums[-1].pair)
        down_line.across()
        down_line.out()
    for one in sums:
        one.back()
    gate_full = assemble(gate_weight, gate_straight, gate_line, False)
    up_full = assemble(up_weight, up_straight, up_line, False)
    down_full = assemble(down_weight, down_straight, down_line, True)
    hidden = input_wide + resid_scale * jnp.concatenate([one.value() for one in sums], axis=0).astype(wide)

    scale_ffn = lax.rsqrt(jnp.mean(hidden * hidden, axis=-1, keepdims=True) + norm_eps)
    unit_ffn = hidden * scale_ffn
    normed_ffn = (unit_ffn * ffn_gain_full).astype(low)
    gate_pre = matmul(normed_ffn, gate_full)
    up_proj = matmul(normed_ffn, up_full)
    activation = (gate_pre * jax.nn.sigmoid(gate_pre) * up_proj).astype(low)

    sums_line = LineSum(clock)
    arrivals, keeps = [], []

    def blocks_of(values):
        return [values[:, s * block : (s + 1) * block] for s in range(cp_count)]

    def send(product, model_side, other_side):
        arrivals.append(
            [
                cp_deliver(
                    lane,
                    clock.run(lambda m, o: product(m, o).astype(low), model_side[s], other_side),
                    s,
                )
                for s in range(1, cp_count)
            ]
        )
        keeps.append((product, model_side[0], other_side))

    def arrive():
        index = sum(part is not None for part in sums_line.parts)
        product, model_side, other_side = keeps[index]

        def total(m, o, *got):
            whole = product(m, o)
            for piece in got:
                whole = whole + piece.astype(wide)
            return whole.astype(low)

        sums_line.load(clock.run(total, model_side, other_side, *arrivals[index]))

    model_last = lambda m, o: matmul_tn(o, m)
    model_first = matmul_tn
    upstream = cot_rows.astype(wide)
    down_in = (resid_scale * upstream).astype(low)
    down_in_blocks = blocks_of(down_in)
    hidden_units = activation.shape[1]
    quarter, half = hidden_units // 4, hidden_units // 2
    send(model_last, down_in_blocks, activation[:, : quarter // 2])
    send(model_last, down_in_blocks, activation[:, quarter // 2 : quarter])
    send(model_last, down_in_blocks, activation[:, quarter:half])

    def unit_grads(down_in, down_full, gate_pre, up_proj):
        hidden_grad = matmul_nt(down_in, down_full)
        gate_sig = jax.nn.sigmoid(gate_pre)
        gate_in = hidden_grad * up_proj * gate_sig * (1.0 + gate_pre * (1.0 - gate_sig))
        return gate_in.astype(low), (hidden_grad * gate_pre * gate_sig).astype(low)

    send(model_last, down_in_blocks, activation[:, half:])
    step = sums_line.step
    arrive()
    step()
    arrive()
    step()
    gate_in, upper_in = clock.run(unit_grads, down_in, down_full, gate_pre, up_proj)
    arrive()
    step()
    normed_ffn_blocks = blocks_of(normed_ffn)
    send(model_first, normed_ffn_blocks, gate_in[:, :half])
    arrive()
    step()
    ffn_sum = TpTotal(
        clock.run(
            lambda a, b, c, d: matmul_nt(a, b) + matmul_nt(c, d), gate_in, gate_full, upper_in, up_full
        )
    )
    send(model_first, normed_ffn_blocks, gate_in[:, half:])
    ffn_sum.across(*clock.last)
    arrive()
    step()
    send(model_first, normed_ffn_blocks, upper_in[:, :half])
    ffn_sum.back(*clock.last)

    def hidden_grads(ffn_norm_grad, hidden, scale_ffn, upstream, ffn_gain_full):
        ffn_norm_grad = ffn_norm_grad.astype(wide)
        unit_ffn = hidden * scale_ffn
        hidden_back = upstream + norm_back(ffn_norm_grad, unit_ffn, scale_ffn, ffn_gain_full)
        return (
            (resid_scale * hidden_back).astype(low),
            hidden_back,
            jnp.sum(ffn_norm_grad * unit_ffn, axis=0),
        )

    attn_in, hidden_back, ffn_gain_part = clock.run(
        hidden_grads, ffn_sum.value(), hidden, scale_ffn, upstream, ffn_gain_full
    )
    attn_in_blocks = blocks_of(attn_in)
    mix_grad = clock.run(lambda a, b: matmul_nt(a, b).astype(low), attn_in, out_full)

    def attention_grads(tree):
        here = slice(tree * rows, (tree + 1) * rows)
        lse = lses[tree][:, ::HD].T.reshape(-1, 2, rows)
        dq, dk, dv = clock.run(
            lambda grad, q, kv, lse: attend_back(
                q,
                kv[:, :kv_width],
                kv[:, kv_width:],
                grad,
                lse,
                row_meta_t[tree],
                key_meta_t[tree],
                per_kv,
            ),
            mix_grad[here],
            query_low[here],
            kv_sets[tree],
            lse,
        )
        dkv = jnp.concatenate([dk, dv], axis=1)
        got = [
            cp_deliver(lane, dkv[s * rows : (s + 1) * rows].astype(low), s)
            for s in range(1, cp_count)
        ]
        return dq, dkv[:rows], got

    tree_grads = [attention_grads(0)]
    arrive()
    step()
    tree_grads += [attention_grads(tree) for tree in range(1, trees)]
    send(model_first, normed_ffn_blocks, upper_in[:, half:])
    arrive()
    step()
    send(model_last, attn_in_blocks, mixture_all)

    def qkv_grads(cos_qk, sin_qk, *parts):
        queries, own, got = parts[:trees], parts[trees : 2 * trees], parts[2 * trees :]
        each = len(got) // trees
        sums = []
        for tree in range(trees):
            total = own[tree]
            for piece in got[tree * each : (tree + 1) * each]:
                total = total + piece.astype(wide)
            sums.append(total)
        kv_turned = jnp.concatenate(sums, axis=0)
        qk_turned = jnp.concatenate(
            [jnp.concatenate(queries, axis=0), kv_turned[:, :kv_width]], axis=1
        )
        qk_in = qk_turned * cos_qk - turn(qk_turned) * sin_qk
        return jnp.concatenate([qk_in, kv_turned[:, kv_width:]], axis=1).astype(low)

    qkv_in = clock.run(
        qkv_grads,
        cos_qk,
        sin_qk,
        *[g[0] for g in tree_grads],
        *[g[1] for g in tree_grads],
        *[piece for g in tree_grads for piece in g[2]],
    )
    normed_attn_blocks = blocks_of(normed_attn)
    send(model_last, normed_attn_blocks, qkv_in[:, :q_width])
    arrive()
    step()
    attn_sum = TpTotal(clock.run(matmul_nt, qkv_in, qkv_full))
    send(model_last, normed_attn_blocks, qkv_in[:, q_width:])
    attn_sum.across(*clock.last)
    arrive()
    step()
    attn_sum.back(*clock.last)

    def input_grads(attn_norm_grad, input_wide, scale_attn, hidden_back, attn_gain_full):
        attn_norm_grad = attn_norm_grad.astype(wide)
        unit_attn = input_wide * scale_attn
        input_back = hidden_back + norm_back(attn_norm_grad, unit_attn, scale_attn, attn_gain_full)
        return width_part(input_back, tp_here), jnp.sum(attn_norm_grad * unit_attn, axis=0)

    arrive()
    step()
    input_mine, attn_gain_part = clock.run(
        input_grads, attn_sum.value(), input_wide, scale_attn, hidden_back, attn_gain_full
    )
    gain_rows = 16
    gain_part = jnp.concatenate(
        [attn_gain_part[None], ffn_gain_part[None], jnp.zeros((gain_rows - 2, model_width), wide)]
    )
    send(lambda m, o: m, blocks_of(gain_part), gain_part)
    arrive()
    step()
    down_mine = tp_scatter(clock.run(matmul, activation, down_full))
    result = (width_part(hidden, tp_here) + resid_scale * down_mine).astype(low)
    arrive()
    step()
    for _ in range(LineSum.lag):
        sums_line.load(None)
        step()
    finals = [sums_line.final(index) for index in range(len(keeps))]
    down_grad = jnp.concatenate(finals[0:4], axis=0)
    gate_grad = jnp.concatenate(finals[4:6], axis=1)
    up_grad = jnp.concatenate(finals[6:8], axis=1)
    out_grad, query_grad, kv_grad, gain_grads = finals[8], finals[9].T, finals[10].T, finals[11]
    return (
        result.reshape(inputs.shape),
        input_mine.reshape(inputs.shape),
        gain_grads[0],
        query_grad,
        kv_grad[:, :kv_width],
        kv_grad[:, kv_width:],
        out_grad,
        gain_grads[1],
        gate_grad,
        up_grad,
        down_grad,
    )


def solution(mesh):
    in_specs = (
        P("grp", "cp", "tp"),
        P("grp", "cp", "tp"),
        P("cp"),
        P("cp", "tp"),
        P("cp", "tp"),
        P("cp", "tp"),
        P("tp", "cp"),
        P("cp"),
        P("cp", "tp"),
        P("cp", "tp"),
        P("tp", "cp"),
        P("grp", None),
        P("grp", None),
        P("grp", None),
        P("grp", None),
    )
    out_specs = (
        P("grp", "cp", "tp"),
        P("grp", "cp", "tp"),
        P("cp"),
        P("cp", "tp"),
        P("cp", "tp"),
        P("cp", "tp"),
        P("tp", "cp"),
        P("cp"),
        P("cp", "tp"),
        P("cp", "tp"),
        P("tp", "cp"),
    )
    return jax.shard_map(
        per_device, mesh=mesh, in_specs=in_specs, out_specs=out_specs, check_vma=False
    )
```

```python
import functools
import math

import jax
import jax.numpy as jnp
from jax import lax
from jax.experimental import pallas as pl
from jax.experimental.pallas import tpu as pltpu
from jax.sharding import PartitionSpec as P

HD = 64

norm_eps = 1e-05
att_scale = 0.015625
resid_scale = 0.22
rope_base = 10000000.0
masked_score = -1e30

low = jnp.bfloat16
wide = jnp.float32


def tie(value, *earlier):
    return lax.optimization_barrier((value,) + earlier)[0] if earlier else value


class Lane:
    def __init__(self, depth):
        self.depth = depth
        self.done = []

    def move(self, block, axis, pairs, *earlier):
        if len(self.done) >= self.depth:
            earlier = (self.done[-self.depth],) + earlier
        self.done.append(lax.ppermute(tie(block, *earlier), axis, pairs))
        return self.done[-1]


class Clock:
    def __init__(self):
        self.last = ()

    def run(self, function, *given):
        given = lax.optimization_barrier(given + self.last)[: len(given)]
        result = function(*given)
        self.last = (jax.tree.leaves(result)[0],)
        return result


def cp_fetch(lane, block):
    count = lax.axis_size("cp")
    return [
        lane.move(block, "cp", [((i + s) % count, i) for i in range(count)])
        for s in range(1, count)
    ]


def cp_deliver(lane, block, shift):
    count = lax.axis_size("cp")
    return lane.move(block, "cp", [(i, (i + shift) % count) for i in range(count)])


def in_order(flag, first, second):
    return [jnp.where(flag, first, second), jnp.where(flag, second, first)]


class LineGather:
    def __init__(self, block):
        self.right, self.left = [block], [block]

    def step(self, *earlier):
        last = lax.axis_size("grp") - 1
        self.right.append(
            lax.ppermute(tie(self.right[-1], *earlier), "grp", [(i, i + 1) for i in range(last)])
        )
        self.left.append(
            lax.ppermute(tie(self.left[-1], *earlier), "grp", [(i + 1, i) for i in range(last)])
        )

    def got(self):
        return self.right[-1], self.left[-1]


def assemble_kernel(here_ref, own_ref, *refs, own_blocks, share_blocks, beside):
    step, here = pl.program_id(0), here_ref[0]
    share_ref, *moved_refs, out_ref = refs
    width = own_ref.shape[1]
    place = step if beside else step - own_blocks
    target = out_ref.at[:, width:] if beside else out_ref
    if beside:
        out_ref[:, :width] = own_ref[...]
    else:

        @pl.when(place < 0)
        def _():
            target[...] = own_ref[...]

    owner = lax.div(jnp.maximum(place, 0), share_blocks)
    away = len(moved_refs) // 2
    for shift, ref in zip([0, *range(1, away + 1), *range(-1, -away - 1, -1)], [share_ref, *moved_refs]):

        @pl.when((place >= 0) & (owner == here - shift))
        def _():
            target[...] = ref[...]


def assemble_shared(weight, line, beside):
    share = line.right[0].shape[0]
    rows, width = weight.shape
    unit = math.gcd(rows, share)
    own_blocks, share_blocks = rows // unit, share // unit
    offset = 0 if beside else own_blocks
    spec = lambda first, count: pl.BlockSpec(
        (unit, width), lambda i, here: (jnp.clip(i - first(here[0]), 0, count - 1), 0)
    )
    moved = lambda shift: spec(lambda z: offset + (z - shift) * share_blocks, share_blocks)
    away = len(line.right) - 1
    specs = [spec(lambda z: 0, own_blocks)]
    specs += [moved(shift) for shift in [*range(away + 1), *range(-1, -away - 1, -1)]]
    out_shape = (rows, 2 * width) if beside else (2 * rows, width)
    return pl.pallas_call(
        functools.partial(
            assemble_kernel, own_blocks=own_blocks, share_blocks=share_blocks, beside=beside
        ),
        grid_spec=pltpu.PrefetchScalarGridSpec(
            num_scalar_prefetch=1,
            grid=(out_shape[0] // unit,),
            in_specs=specs,
            out_specs=pl.BlockSpec((unit, out_shape[1]), lambda i, here: (i, 0)),
        ),
        out_shape=jax.ShapeDtypeStruct(out_shape, weight.dtype),
        cost_estimate=pl.CostEstimate(
            flops=0, bytes_accessed=8 * rows * width + 2 * share * width, transcendentals=0
        ),
        name="assemble",
    )(
        lax.axis_index("grp").astype(jnp.int32).reshape(1),
        weight,
        *line.right,
        *line.left[1:],
    )


class LineSum:
    lag = 3

    def __init__(self, clock):
        here = lax.axis_index("grp")
        self.inner = (here == 1) | (here == 2)
        self.clock = clock
        self.parts, self.sums, self.totals = [], [], []
        self.ins, self.acrosses, self.outs, self.loads = [], [], [], []

    def load(self, part):
        self.parts.append(part)
        back = len(self.parts) - 1 - self.lag
        total = self.totals[back] if back >= 0 else None
        if part is None or total is None or part.shape[1] != total.shape[1]:
            self.loads.append((part, total))
            return
        height = max(part.shape[0], total.shape[0])

        def choose(part, total):
            fill = lambda v: jnp.pad(v, ((0, height - v.shape[0]), (0, 0)))
            return jnp.where(self.inner, fill(total), fill(part))

        self.loads.append(self.clock.run(choose, part, total))

    def step(self):
        count = len(self.loads) - 1
        before = self.ins[-1:] + self.outs[-1:]
        load = self.loads[count]
        if isinstance(load, tuple):
            part, total = load
            if part is not None:
                self.ins.append(lax.ppermute(tie(part, *before), "grp", [(0, 1), (3, 2)]))
            if total is not None:
                self.outs.append(lax.ppermute(tie(total, *before), "grp", [(1, 0), (2, 3)]))
        else:
            side = lax.ppermute(tie(load, *before), "grp", [(0, 1), (1, 0), (2, 3), (3, 2)])
            self.ins.append(side)
            self.outs.append(side)
        if count >= 1 and self.parts[count - 1] is not None:
            part, got = self.parts[count - 1], self.ins[count - 1]
            total = self.clock.run(lambda p, g: p + g[: p.shape[0]], part, got)
            self.sums.append(total)
            self.acrosses.append(
                lax.ppermute(tie(total, *self.acrosses[-1:]), "grp", [(1, 2), (2, 1)])
            )
        if count >= 2 and self.parts[count - 2] is not None:
            self.totals.append(
                self.clock.run(lambda a, b: a + b, self.sums[count - 2], self.acrosses[count - 2])
            )

    def final(self, index):
        total, got = self.totals[index], self.outs[index]
        return jnp.where(self.inner, total, got[: total.shape[0]]).astype(wide)


def tp_swap(block, bit, *earlier):
    count = lax.axis_size("tp")
    return lax.ppermute(tie(block, *earlier), "tp", [(i, i ^ bit) for i in range(count)])


class TpTotal:
    def __init__(self, part):
        self.plain = None
        if lax.axis_size("tp") != 4:
            self.plain = lax.psum(part.astype(low), "tp")
            return
        half = part.shape[0] // 2
        self.odd = lax.axis_index("tp") % 2
        self.mine = lax.dynamic_slice_in_dim(part, self.odd * half, half, 0)
        theirs = lax.dynamic_slice_in_dim(part, (1 - self.odd) * half, half, 0)
        self.got = tp_swap(theirs.astype(low), 1)

    def across(self, *earlier):
        if self.plain is None:
            self.pair = (self.mine.astype(wide) + self.got.astype(wide)).astype(low)
            self.far = tp_swap(self.pair, 2, *earlier)
            return self.far
        return self.plain

    def back(self, *earlier):
        if self.plain is None:
            self.total = (self.pair.astype(wide) + self.far.astype(wide)).astype(low)
            self.other = tp_swap(self.total, 1, *earlier)
            return self.other
        return self.plain

    def value(self):
        if self.plain is None:
            return jnp.concatenate(in_order(self.odd == 0, self.total, self.other), axis=0)
        return self.plain


def attend_kernel(
    q_ref, k_ref, v_ref, row_ref, col_ref, o_ref, lse_ref, bias_ref, *, per_kv
):
    step = pl.program_id(0)
    group = (2 * step) // per_kv

    @pl.when(step == 0)
    def _():
        seg, par, grand, pos = (row_ref[:, i : i + 1] for i in range(4))
        key_seg, key_pos = col_ref[0:1, :], col_ref[1:2, :]
        linked = (key_seg == seg) | (key_seg == par) | (key_seg == grand)
        bias_ref[...] = jnp.where(linked & (key_pos <= pos), 0.0, masked_score)

    k = jnp.where(group == 0, k_ref[:, :HD], k_ref[:, HD : 2 * HD])
    v = jnp.where(group == 0, v_ref[:, :HD], v_ref[:, HD : 2 * HD])
    outs, totals = [], []
    for h in range(2):
        q = q_ref[:, h * HD : (h + 1) * HD]
        s = lax.dot_general(q, k, (((1,), (1,)), ((), ())), preferred_element_type=wide)
        s = s + bias_ref[...]
        top = jnp.max(s, axis=-1, keepdims=True)
        p = jnp.exp(s - top)
        norm = jnp.sum(p, axis=-1, keepdims=True)
        o = jnp.dot(p.astype(low), v, preferred_element_type=wide)
        outs.append(o / norm)
        totals.append(top + jnp.log(norm))
    o_ref[...] = jnp.concatenate(outs, axis=1).astype(low)
    lse_ref[...] = jnp.concatenate([jnp.broadcast_to(t, (t.shape[0], HD)) for t in totals], axis=1)


def attend(q, k, v, row_meta, col_meta, per_kv):
    rows, width = q.shape
    keys, kv_width = k.shape
    pairs = width // (2 * HD)
    whole = lambda a: pl.BlockSpec(a.shape, lambda j: (0, 0))
    tile = pl.BlockSpec((rows, 2 * HD), lambda j: (0, j))
    heads = 2 * pairs
    return pl.pallas_call(
        functools.partial(attend_kernel, per_kv=per_kv),
        grid=(pairs,),
        in_specs=[tile, whole(k), whole(v), whole(row_meta), whole(col_meta)],
        out_specs=[tile, tile],
        out_shape=[
            jax.ShapeDtypeStruct((rows, width), low),
            jax.ShapeDtypeStruct((rows, width), wide),
        ],
        scratch_shapes=[pltpu.VMEM((rows, keys), wide)],
        cost_estimate=pl.CostEstimate(
            flops=16 * heads * rows * keys * HD,
            bytes_accessed=8 * rows * width + 4 * keys * kv_width,
            transcendentals=heads * rows * keys,
        ),
        name="attend",
    )(q, k, v, row_meta, col_meta)


def attend_back_kernel(
    q_ref, k_ref, v_ref, g_ref, lse_ref, row_ref, col_ref, dq_ref, dk_ref, dv_ref, bias_ref, dk_sum, dv_sum, *, per_kv
):
    step = pl.program_id(0)
    group = (2 * step) // per_kv
    pairs_kv = per_kv // 2

    @pl.when(step == 0)
    def _():
        seg, par, grand, pos = (row_ref[i : i + 1, :] for i in range(4))
        key_seg, key_pos = col_ref[:, 0:1], col_ref[:, 1:2]
        linked = (key_seg == seg) | (key_seg == par) | (key_seg == grand)
        bias_ref[...] = jnp.where(linked & (key_pos <= pos), 0.0, masked_score)

    k = jnp.where(group == 0, k_ref[:, :HD], k_ref[:, HD : 2 * HD])
    v = jnp.where(group == 0, v_ref[:, :HD], v_ref[:, HD : 2 * HD])
    outs = []
    dk = jnp.zeros(k.shape, wide)
    dv = jnp.zeros(k.shape, wide)
    nt = (((1,), (1,)), ((), ()))
    for h in range(2):
        q = q_ref[:, h * HD : (h + 1) * HD]
        g = g_ref[:, h * HD : (h + 1) * HD]
        s = lax.dot_general(k, q, nt, preferred_element_type=wide) + bias_ref[...]
        p = jnp.exp(s - lse_ref[0, h : h + 1, :])
        dp = lax.dot_general(v, g, nt, preferred_element_type=wide)
        dv = dv + jnp.dot(p.astype(low), g, preferred_element_type=wide)
        mean = jnp.sum(p * dp, axis=0, keepdims=True)
        dz = (p * (dp - mean)).astype(low)
        dk = dk + jnp.dot(dz, q, preferred_element_type=wide)
        dq = lax.dot_general(dz, k, (((0,), (0,)), ((), ())), preferred_element_type=wide)
        outs.append(dq * att_scale)
    dq_ref[...] = jnp.concatenate(outs, axis=1)
    first = lax.rem(step, pairs_kv) == 0

    @pl.when(first)
    def _():
        dk_sum[...] = dk
        dv_sum[...] = dv

    @pl.when(jnp.logical_not(first))
    def _():
        dk_sum[...] += dk
        dv_sum[...] += dv

    for which in range(2):

        @pl.when(step == (which + 1) * pairs_kv - 1)
        def _():
            dk_ref[:, which * HD : (which + 1) * HD] = dk_sum[...]
            dv_ref[:, which * HD : (which + 1) * HD] = dv_sum[...]


def attend_back(q, k, v, g, lse, row_meta, col_meta, per_kv):
    rows, width = q.shape
    keys, kv_width = k.shape
    pairs = width // (2 * HD)
    heads = 2 * pairs
    whole = lambda a: pl.BlockSpec(a.shape, lambda j: (0, 0))
    tile = pl.BlockSpec((rows, 2 * HD), lambda j: (0, j))
    return pl.pallas_call(
        functools.partial(attend_back_kernel, per_kv=per_kv),
        grid=(pairs,),
        in_specs=[
            tile,
            whole(k),
            whole(v),
            tile,
            pl.BlockSpec((1, 2, rows), lambda j: (j, 0, 0)),
            whole(row_meta),
            whole(col_meta),
        ],
        out_specs=[tile, whole(k), whole(v)],
        out_shape=[
            jax.ShapeDtypeStruct((rows, width), wide),
            jax.ShapeDtypeStruct((keys, kv_width), wide),
            jax.ShapeDtypeStruct((keys, kv_width), wide),
        ],
        scratch_shapes=[
            pltpu.VMEM((keys, rows), wide),
            pltpu.VMEM((keys, HD), wide),
            pltpu.VMEM((keys, HD), wide),
        ],
        cost_estimate=pl.CostEstimate(
            flops=40 * heads * rows * keys * HD,
            bytes_accessed=8 * rows * width + 12 * keys * kv_width,
            transcendentals=heads * rows * keys,
        ),
        name="attend_back",
    )(q, k, v, g, lse, row_meta, col_meta)


def rope_tables(position, repeats):
    half_dim = HD // 2
    freq_index = jnp.arange(half_dim, dtype=wide)
    inverse = jnp.power(wide(rope_base), freq_index * (-2.0 / HD))
    angles = position.astype(wide)[:, None] * inverse
    tile = lambda table: jnp.tile(table, (1, 2 * repeats))
    return tile(jnp.cos(angles)), tile(jnp.sin(angles))


def turn(values):
    half_dim = HD // 2
    front = lax.broadcasted_iota(jnp.int32, values.shape, 1) % HD < half_dim
    return jnp.where(
        front, -jnp.roll(values, -half_dim, axis=1), jnp.roll(values, half_dim, axis=1)
    )


def norm_back(norm_grad, normed_unit, inv_scale, gain_vec):
    scaled = norm_grad * gain_vec
    return inv_scale * (
        scaled - normed_unit * jnp.mean(scaled * normed_unit, axis=-1, keepdims=True)
    )


def matmul(a, b):
    return jnp.dot(a, b, preferred_element_type=wide)


def matmul_nt(a, b):
    return lax.dot_general(a, b, (((1,), (1,)), ((), ())), preferred_element_type=wide)


def matmul_tn(a, b):
    return lax.dot_general(a, b, (((0,), (0,)), ((), ())), preferred_element_type=wide)


def tree_segments(seg_parent, seg_start, seg_len, key_count):
    token_ids = jnp.arange(key_count, dtype=jnp.int32)
    slot_ids = jnp.arange(seg_parent.shape[1], dtype=jnp.int32)
    member = (token_ids[None, :, None] >= seg_start[:, None, :]) & (
        token_ids[None, :, None] < (seg_start + seg_len)[:, None, :]
    )
    pick = lambda table: jnp.sum(jnp.where(member, table[:, None, :], 0), axis=2)
    grand_parent = jnp.sum(
        jnp.where(seg_parent[:, :, None] == slot_ids[None, None, :], seg_parent[:, None, :], 0),
        axis=2,
    )
    return (
        pick(jnp.broadcast_to(slot_ids[None, :], seg_parent.shape)),
        pick(seg_parent),
        pick(grand_parent),
    )


def per_device(
    inputs,
    cotangent,
    attn_gain,
    query_weight,
    key_weight,
    value_weight,
    out_weight,
    ffn_gain,
    gate_weight,
    up_weight,
    down_weight,
    seg_parent,
    seg_start,
    seg_len,
    positions,
):
    trees, rows, part_width = inputs.shape
    keys = positions.shape[1]
    block = attn_gain.shape[0]
    cp_count, tp_count, grp_count = lax.axis_size("cp"), lax.axis_size("tp"), lax.axis_size("grp")
    model_width = block * cp_count
    q_width, kv_width = query_weight.shape[1], key_weight.shape[1]
    per_kv = q_width // kv_width
    tokens = trees * rows
    cp_here, tp_here = lax.axis_index("cp"), lax.axis_index("tp")

    def rolled(values):
        return lax.dynamic_slice_in_dim(
            jnp.concatenate([values, values], axis=-1), cp_here * block, model_width, values.ndim - 1
        )

    def width_part(values, owner):
        start = (owner * part_width - cp_here * block) % model_width
        if block % part_width:
            values = jnp.concatenate([values, values], axis=-1)
        return lax.dynamic_slice_in_dim(values, start, part_width, 1)

    def tp_width(shard, *earlier):
        shard = tie(shard.reshape(tokens, part_width), *earlier)
        if tp_count != 4:
            return rolled(lax.all_gather(shard, "tp", axis=1, tiled=True)), shard
        far = tp_swap(shard, 2)
        near = tp_swap(jnp.stack([shard, far]), 1)
        pieces = [shard, near[0], far, near[1]]
        picks = [lax.select_n(tp_here, *[pieces[j ^ m] for m in range(4)]) for j in range(4)]
        return rolled(jnp.concatenate(picks, axis=1)), far

    def tp_scatter(part):
        if tp_count != 4:
            natural = lax.dynamic_slice_in_dim(
                jnp.concatenate([part, part], axis=-1),
                (model_width - cp_here * block) % model_width,
                model_width,
                1,
            )
            return lax.psum_scatter(
                natural.astype(low), "tp", scatter_dimension=1, tiled=True
            ).astype(wide)
        sent = jnp.concatenate([width_part(part, tp_here ^ 1), width_part(part, tp_here ^ 3)], axis=1)
        got = tp_swap(sent.astype(low), 1).astype(wide)
        kept = width_part(part, tp_here) + got[:, :part_width]
        passed = width_part(part, tp_here ^ 2) + got[:, part_width:]
        return kept + tp_swap(passed.astype(low), 2).astype(wide)

    free, lane = Lane(64), Lane(2)
    shared = cp_count == 2 and grp_count == 4

    def share_of(weight, *earlier):
        if not shared:
            return None
        share = weight.shape[0] // grp_count
        part = lax.dynamic_slice_in_dim(weight, lax.axis_index("grp") * share, share, 0)
        return LineGather(cp_fetch(free, tie(part, *earlier))[0])

    def assemble(weight, others, gathered, beside):
        if shared:
            return assemble_shared(weight, gathered, beside)
        return jnp.concatenate([weight] + others, axis=1 if beside else 0)

    qkv_own = jnp.concatenate([query_weight, key_weight, value_weight], axis=1)
    gains_own = jnp.stack([attn_gain, ffn_gain])
    qkv_others = cp_fetch(free, qkv_own)
    gains = jnp.concatenate([gains_own] + cp_fetch(free, gains_own), axis=1).astype(wide)
    attn_gain_full, ffn_gain_full = gains[0:1], gains[1:2]
    qkv_full = jnp.concatenate([qkv_own] + qkv_others, axis=0)
    input_rows, input_far = tp_width(inputs)
    input_rows = tie(input_rows, *qkv_others)
    gate_line = share_of(gate_weight)
    cot_rows, _ = tp_width(cotangent, input_far)

    seg, parent, grand = tree_segments(seg_parent, seg_start, seg_len, keys)
    meta = jnp.stack([seg, parent, grand, positions], axis=1)
    first_row = cp_here * rows
    row_meta_t = lax.dynamic_slice_in_dim(meta, first_row, rows, 2)
    key_meta = lax.dynamic_slice_in_dim(
        jnp.concatenate([meta[:, 0::3], meta[:, 0::3]], axis=2), first_row, keys, 2
    )
    row_meta = jnp.swapaxes(row_meta_t, 1, 2)
    key_meta_t = jnp.swapaxes(key_meta, 1, 2)
    own_pos = row_meta_t[:, 3].reshape(tokens)
    cos_qk, sin_qk = rope_tables(own_pos, (q_width + kv_width) // HD)

    input_wide = input_rows.astype(wide)
    scale_attn = lax.rsqrt(jnp.mean(input_wide * input_wide, axis=-1, keepdims=True) + norm_eps)
    unit_attn = input_wide * scale_attn
    normed_attn = (unit_attn * attn_gain_full).astype(low)
    qkv_raw = matmul(normed_attn, qkv_full)
    qk_raw = qkv_raw[:, : q_width + kv_width]
    qk_rot = qk_raw * cos_qk + turn(qk_raw) * sin_qk
    query_low = qk_rot[:, :q_width].astype(low) * low(att_scale)
    key_low = qk_rot[:, q_width:].astype(low)
    kv_own = jnp.concatenate([key_low, qkv_raw[:, q_width + kv_width :].astype(low)], axis=1)
    kv_sets = [
        jnp.concatenate([own] + cp_fetch(free, own), axis=0)
        for own in (kv_own[t * rows : (t + 1) * rows] for t in range(trees))
    ]
    out_others = cp_fetch(free, tie(out_weight, query_low))
    out_full = jnp.concatenate([out_weight] + out_others, axis=1)
    clock = Clock()
    mixtures, lses, sums = [], [], []
    if shared:
        gate_line.step(query_low)
    for tree in range(trees):
        here = slice(tree * rows, (tree + 1) * rows)
        mixture, lse = clock.run(
            lambda q, kv, *_: attend(
                q, kv[:, :kv_width], kv[:, kv_width:], row_meta[tree], key_meta[tree], per_kv
            ),
            query_low[here],
            kv_sets[tree],
            cot_rows,
        )
        mixtures.append(mixture)
        lses.append(lse)
    gate_first = gate_line.got() if shared else ()
    for mixture in mixtures:
        sums.append(TpTotal(clock.run(lambda a, b, *_: matmul(a, b), mixture, out_full, *gate_first)))
    mixture_all = jnp.concatenate(mixtures, axis=0)
    if shared:
        gate_line.step()
    half_rows = up_weight.shape[0] // 2
    up_top = cp_fetch(free, tie(up_weight[:half_rows], *kv_sets, *out_others))
    for one in sums:
        one.across()
    gate_second = gate_line.got() if shared else ()
    sums[0].back(*gate_second)
    for one in sums[1:]:
        one.back(*gate_second, *up_top)
    up_bottom = cp_fetch(free, tie(up_weight[half_rows:], *up_top))
    up_others = [piece for pair in zip(up_top, up_bottom) for piece in pair]
    if shared:
        gate_line.step()
    down_line = share_of(down_weight, *up_top)
    gate_others = [] if shared else cp_fetch(free, gate_weight)
    down_others = [] if shared else cp_fetch(free, down_weight)
    gate_full = clock.run(lambda w: assemble(w, gate_others, gate_line, False), gate_weight)
    hidden = input_wide + resid_scale * jnp.concatenate([one.value() for one in sums], axis=0).astype(wide)

    scale_ffn = lax.rsqrt(jnp.mean(hidden * hidden, axis=-1, keepdims=True) + norm_eps)
    unit_ffn = hidden * scale_ffn
    normed_ffn = (unit_ffn * ffn_gain_full).astype(low)
    gate_pre = clock.run(matmul, normed_ffn, gate_full)
    up_proj = clock.run(matmul, normed_ffn[:, :block], up_weight)
    for index, piece in enumerate(up_others):
        first = block + index * half_rows
        up_proj = up_proj + matmul(normed_ffn[:, first : first + half_rows], piece)
    up_full = jnp.concatenate([up_weight] + up_others, axis=0)
    activation = (gate_pre * jax.nn.sigmoid(gate_pre) * up_proj).astype(low)
    if shared:
        for _ in range(grp_count - 1):
            down_line.step()
    down_full = assemble(down_weight, down_others, down_line, True)

    sums_line = LineSum(clock)
    arrivals, keeps = [], []

    def blocks_of(values):
        return [values[:, s * block : (s + 1) * block] for s in range(cp_count)]

    def send(product, model_side, other_side):
        arrivals.append(
            [
                cp_deliver(
                    lane,
                    clock.run(lambda m, o: product(m, o).astype(low), model_side[s], other_side),
                    s,
                )
                for s in range(1, cp_count)
            ]
        )
        keeps.append((product, model_side[0], other_side))

    def arrive():
        index = sum(part is not None for part in sums_line.parts)
        product, model_side, other_side = keeps[index]

        def total(m, o, *got):
            whole = product(m, o)
            for piece in got:
                whole = whole + piece.astype(wide)
            return whole.astype(low)

        sums_line.load(clock.run(total, model_side, other_side, *arrivals[index]))

    model_last = lambda m, o: matmul_tn(o, m)
    model_first = matmul_tn
    upstream = cot_rows.astype(wide)
    down_in = (resid_scale * upstream).astype(low)
    down_in_blocks = blocks_of(down_in)
    hidden_units = activation.shape[1]
    quarter, half = hidden_units // 4, hidden_units // 2
    send(model_last, down_in_blocks, activation[:, : quarter // 2])
    send(model_last, down_in_blocks, activation[:, quarter // 2 : quarter])
    send(model_last, down_in_blocks, activation[:, quarter:half])

    def unit_grads(down_in, down_full, gate_pre, up_proj):
        hidden_grad = matmul_nt(down_in, down_full)
        gate_sig = jax.nn.sigmoid(gate_pre)
        gate_in = hidden_grad * up_proj * gate_sig * (1.0 + gate_pre * (1.0 - gate_sig))
        return gate_in.astype(low), (hidden_grad * gate_pre * gate_sig).astype(low)

    send(model_last, down_in_blocks, activation[:, half:])
    step = sums_line.step
    arrive()
    step()
    arrive()
    step()
    gate_in, upper_in = clock.run(unit_grads, down_in, down_full, gate_pre, up_proj)
    arrive()
    step()
    normed_ffn_blocks = blocks_of(normed_ffn)
    send(model_first, normed_ffn_blocks, gate_in[:, :half])
    arrive()
    step()
    ffn_sum = TpTotal(
        clock.run(
            lambda a, b, c, d: matmul_nt(a, b) + matmul_nt(c, d), gate_in, gate_full, upper_in, up_full
        )
    )
    send(model_first, normed_ffn_blocks, gate_in[:, half:])
    ffn_sum.across(*clock.last)
    arrive()
    step()
    send(model_first, normed_ffn_blocks, upper_in[:, :half])
    ffn_sum.back(*clock.last)

    def hidden_grads(ffn_norm_grad, hidden, scale_ffn, upstream, ffn_gain_full):
        ffn_norm_grad = ffn_norm_grad.astype(wide)
        unit_ffn = hidden * scale_ffn
        hidden_back = upstream + norm_back(ffn_norm_grad, unit_ffn, scale_ffn, ffn_gain_full)
        return (
            (resid_scale * hidden_back).astype(low),
            hidden_back,
            jnp.sum(ffn_norm_grad * unit_ffn, axis=0),
        )

    attn_in, hidden_back, ffn_gain_part = clock.run(
        hidden_grads, ffn_sum.value(), hidden, scale_ffn, upstream, ffn_gain_full
    )
    attn_in_blocks = blocks_of(attn_in)
    mix_grad = clock.run(lambda a, b: matmul_nt(a, b).astype(low), attn_in, out_full)

    def attention_grads(tree):
        here = slice(tree * rows, (tree + 1) * rows)
        lse = lses[tree][:, ::HD].T.reshape(-1, 2, rows)
        dq, dk, dv = clock.run(
            lambda grad, q, kv, lse: attend_back(
                q,
                kv[:, :kv_width],
                kv[:, kv_width:],
                grad,
                lse,
                row_meta_t[tree],
                key_meta_t[tree],
                per_kv,
            ),
            mix_grad[here],
            query_low[here],
            kv_sets[tree],
            lse,
        )
        dkv = jnp.concatenate([dk, dv], axis=1)
        got = [
            cp_deliver(lane, dkv[s * rows : (s + 1) * rows].astype(low), s)
            for s in range(1, cp_count)
        ]
        return dq, dkv[:rows], got

    tree_grads = [attention_grads(0)]
    arrive()
    step()
    tree_grads += [attention_grads(tree) for tree in range(1, trees)]
    send(model_first, normed_ffn_blocks, upper_in[:, half:])
    arrive()
    step()
    send(model_last, attn_in_blocks, mixture_all)

    def qkv_grads(cos_qk, sin_qk, *parts):
        queries, own, got = parts[:trees], parts[trees : 2 * trees], parts[2 * trees :]
        each = len(got) // trees
        sums = []
        for tree in range(trees):
            total = own[tree]
            for piece in got[tree * each : (tree + 1) * each]:
                total = total + piece.astype(wide)
            sums.append(total)
        kv_turned = jnp.concatenate(sums, axis=0)
        qk_turned = jnp.concatenate(
            [jnp.concatenate(queries, axis=0), kv_turned[:, :kv_width]], axis=1
        )
        qk_in = qk_turned * cos_qk - turn(qk_turned) * sin_qk
        return jnp.concatenate([qk_in, kv_turned[:, kv_width:]], axis=1).astype(low)

    qkv_in = clock.run(
        qkv_grads,
        cos_qk,
        sin_qk,
        *[g[0] for g in tree_grads],
        *[g[1] for g in tree_grads],
        *[piece for g in tree_grads for piece in g[2]],
    )
    normed_attn_blocks = blocks_of(normed_attn)
    send(model_last, normed_attn_blocks, qkv_in[:, :q_width])
    arrive()
    step()
    attn_sum = TpTotal(clock.run(matmul_nt, qkv_in, qkv_full))
    send(model_last, normed_attn_blocks, qkv_in[:, q_width:])
    attn_sum.across(*clock.last)
    arrive()
    step()
    attn_sum.back(*clock.last)

    def input_grads(attn_norm_grad, input_wide, scale_attn, hidden_back, attn_gain_full):
        attn_norm_grad = attn_norm_grad.astype(wide)
        unit_attn = input_wide * scale_attn
        input_back = hidden_back + norm_back(attn_norm_grad, unit_attn, scale_attn, attn_gain_full)
        return width_part(input_back, tp_here), jnp.sum(attn_norm_grad * unit_attn, axis=0)

    arrive()
    step()
    input_mine, attn_gain_part = clock.run(
        input_grads, attn_sum.value(), input_wide, scale_attn, hidden_back, attn_gain_full
    )
    gain_rows = 16
    gain_part = jnp.concatenate(
        [attn_gain_part[None], ffn_gain_part[None], jnp.zeros((gain_rows - 2, model_width), wide)]
    )
    send(lambda m, o: m, blocks_of(gain_part), gain_part)
    arrive()
    step()
    down_mine = tp_scatter(clock.run(matmul, activation, down_full))
    result = (width_part(hidden, tp_here) + resid_scale * down_mine).astype(low)
    arrive()
    step()
    for _ in range(LineSum.lag):
        sums_line.load(None)
        step()
    finals = [sums_line.final(index) for index in range(len(keeps))]
    down_grad = jnp.concatenate(finals[0:4], axis=0)
    gate_grad = jnp.concatenate(finals[4:6], axis=1)
    up_grad = jnp.concatenate(finals[6:8], axis=1)
    out_grad, query_grad, kv_grad, gain_grads = finals[8], finals[9].T, finals[10].T, finals[11]
    return (
        result.reshape(inputs.shape),
        input_mine.reshape(inputs.shape),
        gain_grads[0],
        query_grad,
        kv_grad[:, :kv_width],
        kv_grad[:, kv_width:],
        out_grad,
        gain_grads[1],
        gate_grad,
        up_grad,
        down_grad,
    )


def solution(mesh):
    in_specs = (
        P("grp", "cp", "tp"),
        P("grp", "cp", "tp"),
        P("cp"),
        P("cp", "tp"),
        P("cp", "tp"),
        P("cp", "tp"),
        P("tp", "cp"),
        P("cp"),
        P("cp", "tp"),
        P("cp", "tp"),
        P("tp", "cp"),
        P("grp", None),
        P("grp", None),
        P("grp", None),
        P("grp", None),
    )
    out_specs = (
        P("grp", "cp", "tp"),
        P("grp", "cp", "tp"),
        P("cp"),
        P("cp", "tp"),
        P("cp", "tp"),
        P("cp", "tp"),
        P("tp", "cp"),
        P("cp"),
        P("cp", "tp"),
        P("cp", "tp"),
        P("tp", "cp"),
    )
    return jax.shard_map(
        per_device, mesh=mesh, in_specs=in_specs, out_specs=out_specs, check_vma=False
    )
```

```python
import functools
import math

import jax
import jax.numpy as jnp
from jax import lax
from jax.experimental import pallas as pl
from jax.experimental.pallas import tpu as pltpu
from jax.sharding import PartitionSpec as P

HD = 64

norm_eps = 1e-05
att_scale = 0.015625
resid_scale = 0.22
rope_base = 10000000.0
masked_score = -1e30

low = jnp.bfloat16
wide = jnp.float32


def tie(value, *earlier):
    return lax.optimization_barrier((value,) + earlier)[0] if earlier else value


class Lane:
    def __init__(self, depth):
        self.depth = depth
        self.done = []

    def move(self, block, axis, pairs, *earlier):
        if len(self.done) >= self.depth:
            earlier = (self.done[-self.depth],) + earlier
        self.done.append(lax.ppermute(tie(block, *earlier), axis, pairs))
        return self.done[-1]


class Clock:
    def __init__(self):
        self.last = ()

    def run(self, function, *given):
        given = lax.optimization_barrier(given + self.last)[: len(given)]
        result = function(*given)
        self.last = (jax.tree.leaves(result)[0],)
        return result


def cp_fetch(lane, block):
    count = lax.axis_size("cp")
    return [
        lane.move(block, "cp", [((i + s) % count, i) for i in range(count)])
        for s in range(1, count)
    ]


def cp_deliver(lane, block, shift):
    count = lax.axis_size("cp")
    return lane.move(block, "cp", [(i, (i + shift) % count) for i in range(count)])


def in_order(flag, first, second):
    return [jnp.where(flag, first, second), jnp.where(flag, second, first)]


class LineGather:
    def __init__(self, block):
        self.right, self.left = [block], [block]

    def step(self, *earlier):
        last = lax.axis_size("grp") - 1
        self.right.append(
            lax.ppermute(tie(self.right[-1], *earlier), "grp", [(i, i + 1) for i in range(last)])
        )
        self.left.append(
            lax.ppermute(tie(self.left[-1], *earlier), "grp", [(i + 1, i) for i in range(last)])
        )

    def got(self):
        return self.right[-1], self.left[-1]


def assemble_kernel(here_ref, own_ref, *refs, own_blocks, share_blocks, beside):
    step, here = pl.program_id(0), here_ref[0]
    share_ref, *moved_refs, out_ref = refs
    width = own_ref.shape[1]
    place = step if beside else step - own_blocks
    target = out_ref.at[:, width:] if beside else out_ref
    if beside:
        out_ref[:, :width] = own_ref[...]
    else:

        @pl.when(place < 0)
        def _():
            target[...] = own_ref[...]

    owner = lax.div(jnp.maximum(place, 0), share_blocks)
    away = len(moved_refs) // 2
    for shift, ref in zip([0, *range(1, away + 1), *range(-1, -away - 1, -1)], [share_ref, *moved_refs]):

        @pl.when((place >= 0) & (owner == here - shift))
        def _():
            target[...] = ref[...]


def assemble_shared(weight, line, beside):
    share = line.right[0].shape[0]
    rows, width = weight.shape
    unit = math.gcd(rows, share)
    own_blocks, share_blocks = rows // unit, share // unit
    offset = 0 if beside else own_blocks
    spec = lambda first, count: pl.BlockSpec(
        (unit, width), lambda i, here: (jnp.clip(i - first(here[0]), 0, count - 1), 0)
    )
    moved = lambda shift: spec(lambda z: offset + (z - shift) * share_blocks, share_blocks)
    away = len(line.right) - 1
    specs = [spec(lambda z: 0, own_blocks)]
    specs += [moved(shift) for shift in [*range(away + 1), *range(-1, -away - 1, -1)]]
    out_shape = (rows, 2 * width) if beside else (2 * rows, width)
    return pl.pallas_call(
        functools.partial(
            assemble_kernel, own_blocks=own_blocks, share_blocks=share_blocks, beside=beside
        ),
        grid_spec=pltpu.PrefetchScalarGridSpec(
            num_scalar_prefetch=1,
            grid=(out_shape[0] // unit,),
            in_specs=specs,
            out_specs=pl.BlockSpec((unit, out_shape[1]), lambda i, here: (i, 0)),
        ),
        out_shape=jax.ShapeDtypeStruct(out_shape, weight.dtype),
        cost_estimate=pl.CostEstimate(
            flops=0, bytes_accessed=8 * rows * width + 2 * share * width, transcendentals=0
        ),
        name="assemble",
    )(
        lax.axis_index("grp").astype(jnp.int32).reshape(1),
        weight,
        *line.right,
        *line.left[1:],
    )


class LineSum:
    lag = 3

    def __init__(self, clock):
        here = lax.axis_index("grp")
        self.inner = (here == 1) | (here == 2)
        self.clock = clock
        self.parts, self.sums, self.totals = [], [], []
        self.ins, self.acrosses, self.outs, self.loads = [], [], [], []

    def load(self, part):
        self.parts.append(part)
        back = len(self.parts) - 1 - self.lag
        total = self.totals[back] if back >= 0 else None
        if part is None or total is None or part.shape[1] != total.shape[1]:
            self.loads.append((part, total))
            return
        height = max(part.shape[0], total.shape[0])

        def choose(part, total):
            fill = lambda v: jnp.pad(v, ((0, height - v.shape[0]), (0, 0)))
            return jnp.where(self.inner, fill(total), fill(part))

        self.loads.append(self.clock.run(choose, part, total))

    def step(self):
        count = len(self.loads) - 1
        before = self.ins[-1:] + self.outs[-1:]
        load = self.loads[count]
        if isinstance(load, tuple):
            part, total = load
            if part is not None:
                self.ins.append(lax.ppermute(tie(part, *before), "grp", [(0, 1), (3, 2)]))
            if total is not None:
                self.outs.append(lax.ppermute(tie(total, *before), "grp", [(1, 0), (2, 3)]))
        else:
            side = lax.ppermute(tie(load, *before), "grp", [(0, 1), (1, 0), (2, 3), (3, 2)])
            self.ins.append(side)
            self.outs.append(side)
        if count >= 1 and self.parts[count - 1] is not None:
            part, got = self.parts[count - 1], self.ins[count - 1]
            total = self.clock.run(lambda p, g: p + g[: p.shape[0]], part, got)
            self.sums.append(total)
            self.acrosses.append(
                lax.ppermute(tie(total, *self.acrosses[-1:]), "grp", [(1, 2), (2, 1)])
            )
        if count >= 2 and self.parts[count - 2] is not None:
            self.totals.append(
                self.clock.run(lambda a, b: a + b, self.sums[count - 2], self.acrosses[count - 2])
            )

    def final(self, index):
        total, got = self.totals[index], self.outs[index]
        return jnp.where(self.inner, total, got[: total.shape[0]]).astype(wide)


def tp_swap(block, bit, *earlier):
    count = lax.axis_size("tp")
    return lax.ppermute(tie(block, *earlier), "tp", [(i, i ^ bit) for i in range(count)])


class TpTotal:
    def __init__(self, part):
        self.plain = None
        if lax.axis_size("tp") != 4:
            self.plain = lax.psum(part.astype(low), "tp")
            return
        half = part.shape[0] // 2
        self.odd = lax.axis_index("tp") % 2
        self.mine = lax.dynamic_slice_in_dim(part, self.odd * half, half, 0)
        theirs = lax.dynamic_slice_in_dim(part, (1 - self.odd) * half, half, 0)
        self.got = tp_swap(theirs.astype(low), 1)

    def across(self, *earlier):
        if self.plain is None:
            self.pair = (self.mine.astype(wide) + self.got.astype(wide)).astype(low)
            self.far = tp_swap(self.pair, 2, *earlier)
            return self.far
        return self.plain

    def back(self, *earlier):
        if self.plain is None:
            self.total = (self.pair.astype(wide) + self.far.astype(wide)).astype(low)
            self.other = tp_swap(self.total, 1, *earlier)
            return self.other
        return self.plain

    def value(self):
        if self.plain is None:
            return jnp.concatenate(in_order(self.odd == 0, self.total, self.other), axis=0)
        return self.plain


def attend_kernel(
    q_ref, k_ref, v_ref, row_ref, col_ref, o_ref, lse_ref, bias_ref, *, per_kv
):
    step = pl.program_id(0)
    group = (2 * step) // per_kv

    @pl.when(step == 0)
    def _():
        seg, par, grand, pos = (row_ref[:, i : i + 1] for i in range(4))
        key_seg, key_pos = col_ref[0:1, :], col_ref[1:2, :]
        linked = (key_seg == seg) | (key_seg == par) | (key_seg == grand)
        bias_ref[...] = jnp.where(linked & (key_pos <= pos), 0.0, masked_score)

    k = jnp.where(group == 0, k_ref[:, :HD], k_ref[:, HD : 2 * HD])
    v = jnp.where(group == 0, v_ref[:, :HD], v_ref[:, HD : 2 * HD])
    outs, totals = [], []
    for h in range(2):
        q = q_ref[:, h * HD : (h + 1) * HD]
        s = lax.dot_general(q, k, (((1,), (1,)), ((), ())), preferred_element_type=wide)
        s = s + bias_ref[...]
        top = jnp.max(s, axis=-1, keepdims=True)
        p = jnp.exp(s - top)
        norm = jnp.sum(p, axis=-1, keepdims=True)
        o = jnp.dot(p.astype(low), v, preferred_element_type=wide)
        outs.append(o / norm)
        totals.append(top + jnp.log(norm))
    o_ref[...] = jnp.concatenate(outs, axis=1).astype(low)
    lse_ref[...] = jnp.concatenate([jnp.broadcast_to(t, (t.shape[0], HD)) for t in totals], axis=1)


def attend(q, k, v, row_meta, col_meta, per_kv):
    rows, width = q.shape
    keys, kv_width = k.shape
    pairs = width // (2 * HD)
    whole = lambda a: pl.BlockSpec(a.shape, lambda j: (0, 0))
    tile = pl.BlockSpec((rows, 2 * HD), lambda j: (0, j))
    heads = 2 * pairs
    return pl.pallas_call(
        functools.partial(attend_kernel, per_kv=per_kv),
        grid=(pairs,),
        in_specs=[tile, whole(k), whole(v), whole(row_meta), whole(col_meta)],
        out_specs=[tile, tile],
        out_shape=[
            jax.ShapeDtypeStruct((rows, width), low),
            jax.ShapeDtypeStruct((rows, width), wide),
        ],
        scratch_shapes=[pltpu.VMEM((rows, keys), wide)],
        cost_estimate=pl.CostEstimate(
            flops=16 * heads * rows * keys * HD,
            bytes_accessed=8 * rows * width + 4 * keys * kv_width,
            transcendentals=heads * rows * keys,
        ),
        name="attend",
    )(q, k, v, row_meta, col_meta)


def attend_back_kernel(
    q_ref, k_ref, v_ref, g_ref, lse_ref, row_ref, col_ref, dq_ref, dk_ref, dv_ref, bias_ref, dk_sum, dv_sum, *, per_kv
):
    step = pl.program_id(0)
    group = (2 * step) // per_kv
    pairs_kv = per_kv // 2

    @pl.when(step == 0)
    def _():
        seg, par, grand, pos = (row_ref[i : i + 1, :] for i in range(4))
        key_seg, key_pos = col_ref[:, 0:1], col_ref[:, 1:2]
        linked = (key_seg == seg) | (key_seg == par) | (key_seg == grand)
        bias_ref[...] = jnp.where(linked & (key_pos <= pos), 0.0, masked_score)

    k = jnp.where(group == 0, k_ref[:, :HD], k_ref[:, HD : 2 * HD])
    v = jnp.where(group == 0, v_ref[:, :HD], v_ref[:, HD : 2 * HD])
    outs = []
    dk = jnp.zeros(k.shape, wide)
    dv = jnp.zeros(k.shape, wide)
    nt = (((1,), (1,)), ((), ()))
    for h in range(2):
        q = q_ref[:, h * HD : (h + 1) * HD]
        g = g_ref[:, h * HD : (h + 1) * HD]
        s = lax.dot_general(k, q, nt, preferred_element_type=wide) + bias_ref[...]
        p = jnp.exp(s - lse_ref[0, h : h + 1, :])
        dp = lax.dot_general(v, g, nt, preferred_element_type=wide)
        dv = dv + jnp.dot(p.astype(low), g, preferred_element_type=wide)
        mean = jnp.sum(p * dp, axis=0, keepdims=True)
        dz = (p * (dp - mean)).astype(low)
        dk = dk + jnp.dot(dz, q, preferred_element_type=wide)
        dq = lax.dot_general(dz, k, (((0,), (0,)), ((), ())), preferred_element_type=wide)
        outs.append(dq * att_scale)
    dq_ref[...] = jnp.concatenate(outs, axis=1)
    first = lax.rem(step, pairs_kv) == 0

    @pl.when(first)
    def _():
        dk_sum[...] = dk
        dv_sum[...] = dv

    @pl.when(jnp.logical_not(first))
    def _():
        dk_sum[...] += dk
        dv_sum[...] += dv

    for which in range(2):

        @pl.when(step == (which + 1) * pairs_kv - 1)
        def _():
            dk_ref[:, which * HD : (which + 1) * HD] = dk_sum[...]
            dv_ref[:, which * HD : (which + 1) * HD] = dv_sum[...]


def attend_back(q, k, v, g, lse, row_meta, col_meta, per_kv):
    rows, width = q.shape
    keys, kv_width = k.shape
    pairs = width // (2 * HD)
    heads = 2 * pairs
    whole = lambda a: pl.BlockSpec(a.shape, lambda j: (0, 0))
    tile = pl.BlockSpec((rows, 2 * HD), lambda j: (0, j))
    return pl.pallas_call(
        functools.partial(attend_back_kernel, per_kv=per_kv),
        grid=(pairs,),
        in_specs=[
            tile,
            whole(k),
            whole(v),
            tile,
            pl.BlockSpec((1, 2, rows), lambda j: (j, 0, 0)),
            whole(row_meta),
            whole(col_meta),
        ],
        out_specs=[tile, whole(k), whole(v)],
        out_shape=[
            jax.ShapeDtypeStruct((rows, width), wide),
            jax.ShapeDtypeStruct((keys, kv_width), wide),
            jax.ShapeDtypeStruct((keys, kv_width), wide),
        ],
        scratch_shapes=[
            pltpu.VMEM((keys, rows), wide),
            pltpu.VMEM((keys, HD), wide),
            pltpu.VMEM((keys, HD), wide),
        ],
        cost_estimate=pl.CostEstimate(
            flops=40 * heads * rows * keys * HD,
            bytes_accessed=8 * rows * width + 12 * keys * kv_width,
            transcendentals=heads * rows * keys,
        ),
        name="attend_back",
    )(q, k, v, g, lse, row_meta, col_meta)


def rope_tables(position, repeats):
    half_dim = HD // 2
    freq_index = jnp.arange(half_dim, dtype=wide)
    inverse = jnp.power(wide(rope_base), freq_index * (-2.0 / HD))
    angles = position.astype(wide)[:, None] * inverse
    tile = lambda table: jnp.tile(table, (1, 2 * repeats))
    return tile(jnp.cos(angles)), tile(jnp.sin(angles))


def turn(values):
    half_dim = HD // 2
    front = lax.broadcasted_iota(jnp.int32, values.shape, 1) % HD < half_dim
    return jnp.where(
        front, -jnp.roll(values, -half_dim, axis=1), jnp.roll(values, half_dim, axis=1)
    )


def norm_back(norm_grad, normed_unit, inv_scale, gain_vec):
    scaled = norm_grad * gain_vec
    return inv_scale * (
        scaled - normed_unit * jnp.mean(scaled * normed_unit, axis=-1, keepdims=True)
    )


def matmul(a, b):
    return jnp.dot(a, b, preferred_element_type=wide)


def matmul_nt(a, b):
    return lax.dot_general(a, b, (((1,), (1,)), ((), ())), preferred_element_type=wide)


def matmul_tn(a, b):
    return lax.dot_general(a, b, (((0,), (0,)), ((), ())), preferred_element_type=wide)


def tree_segments(seg_parent, seg_start, seg_len, key_count):
    token_ids = jnp.arange(key_count, dtype=jnp.int32)
    slot_ids = jnp.arange(seg_parent.shape[1], dtype=jnp.int32)
    member = (token_ids[None, :, None] >= seg_start[:, None, :]) & (
        token_ids[None, :, None] < (seg_start + seg_len)[:, None, :]
    )
    pick = lambda table: jnp.sum(jnp.where(member, table[:, None, :], 0), axis=2)
    grand_parent = jnp.sum(
        jnp.where(seg_parent[:, :, None] == slot_ids[None, None, :], seg_parent[:, None, :], 0),
        axis=2,
    )
    return (
        pick(jnp.broadcast_to(slot_ids[None, :], seg_parent.shape)),
        pick(seg_parent),
        pick(grand_parent),
    )


def per_device(
    inputs,
    cotangent,
    attn_gain,
    query_weight,
    key_weight,
    value_weight,
    out_weight,
    ffn_gain,
    gate_weight,
    up_weight,
    down_weight,
    seg_parent,
    seg_start,
    seg_len,
    positions,
):
    trees, rows, part_width = inputs.shape
    keys = positions.shape[1]
    block = attn_gain.shape[0]
    cp_count, tp_count, grp_count = lax.axis_size("cp"), lax.axis_size("tp"), lax.axis_size("grp")
    model_width = block * cp_count
    q_width, kv_width = query_weight.shape[1], key_weight.shape[1]
    per_kv = q_width // kv_width
    tokens = trees * rows
    cp_here, tp_here = lax.axis_index("cp"), lax.axis_index("tp")

    def rolled(values):
        return lax.dynamic_slice_in_dim(
            jnp.concatenate([values, values], axis=-1), cp_here * block, model_width, values.ndim - 1
        )

    def width_part(values, owner):
        start = (owner * part_width - cp_here * block) % model_width
        if block % part_width:
            values = jnp.concatenate([values, values], axis=-1)
        return lax.dynamic_slice_in_dim(values, start, part_width, 1)

    def tp_width(shard, *earlier):
        shard = tie(shard.reshape(tokens, part_width), *earlier)
        if tp_count != 4:
            return rolled(lax.all_gather(shard, "tp", axis=1, tiled=True)), shard
        far = tp_swap(shard, 2)
        near = tp_swap(jnp.stack([shard, far]), 1)
        pieces = [shard, near[0], far, near[1]]
        picks = [lax.select_n(tp_here, *[pieces[j ^ m] for m in range(4)]) for j in range(4)]
        return rolled(jnp.concatenate(picks, axis=1)), far

    def tp_scatter(part):
        if tp_count != 4:
            natural = lax.dynamic_slice_in_dim(
                jnp.concatenate([part, part], axis=-1),
                (model_width - cp_here * block) % model_width,
                model_width,
                1,
            )
            return lax.psum_scatter(
                natural.astype(low), "tp", scatter_dimension=1, tiled=True
            ).astype(wide)
        sent = jnp.concatenate([width_part(part, tp_here ^ 1), width_part(part, tp_here ^ 3)], axis=1)
        got = tp_swap(sent.astype(low), 1).astype(wide)
        kept = width_part(part, tp_here) + got[:, :part_width]
        passed = width_part(part, tp_here ^ 2) + got[:, part_width:]
        return kept + tp_swap(passed.astype(low), 2).astype(wide)

    free, lane = Lane(64), Lane(2)
    shared = cp_count == 2 and grp_count == 4

    def share_of(weight, *earlier):
        if not shared:
            return None
        share = weight.shape[0] // grp_count
        part = lax.dynamic_slice_in_dim(weight, lax.axis_index("grp") * share, share, 0)
        return LineGather(cp_fetch(free, tie(part, *earlier))[0])

    def assemble(weight, others, gathered, beside):
        if shared:
            return assemble_shared(weight, gathered, beside)
        return jnp.concatenate([weight] + others, axis=1 if beside else 0)

    qkv_own = jnp.concatenate([query_weight, key_weight, value_weight], axis=1)
    gains_own = jnp.stack([attn_gain, ffn_gain])
    qkv_others = cp_fetch(free, qkv_own)
    gains = jnp.concatenate([gains_own] + cp_fetch(free, gains_own), axis=1).astype(wide)
    attn_gain_full, ffn_gain_full = gains[0:1], gains[1:2]
    qkv_full = jnp.concatenate([qkv_own] + qkv_others, axis=0)
    input_rows, input_far = tp_width(inputs)
    input_rows = tie(input_rows, *qkv_others)
    gate_line = share_of(gate_weight)
    cot_rows, _ = tp_width(cotangent, input_far)

    seg, parent, grand = tree_segments(seg_parent, seg_start, seg_len, keys)
    meta = jnp.stack([seg, parent, grand, positions], axis=1)
    first_row = cp_here * rows
    row_meta_t = lax.dynamic_slice_in_dim(meta, first_row, rows, 2)
    key_meta = lax.dynamic_slice_in_dim(
        jnp.concatenate([meta[:, 0::3], meta[:, 0::3]], axis=2), first_row, keys, 2
    )
    row_meta = jnp.swapaxes(row_meta_t, 1, 2)
    key_meta_t = jnp.swapaxes(key_meta, 1, 2)
    own_pos = row_meta_t[:, 3].reshape(tokens)
    cos_qk, sin_qk = rope_tables(own_pos, (q_width + kv_width) // HD)

    input_wide = input_rows.astype(wide)
    scale_attn = lax.rsqrt(jnp.mean(input_wide * input_wide, axis=-1, keepdims=True) + norm_eps)
    unit_attn = input_wide * scale_attn
    normed_attn = (unit_attn * attn_gain_full).astype(low)
    qkv_raw = matmul(normed_attn, qkv_full)
    qk_raw = qkv_raw[:, : q_width + kv_width]
    qk_rot = qk_raw * cos_qk + turn(qk_raw) * sin_qk
    query_low = qk_rot[:, :q_width].astype(low) * low(att_scale)
    key_low = qk_rot[:, q_width:].astype(low)
    kv_own = jnp.concatenate([key_low, qkv_raw[:, q_width + kv_width :].astype(low)], axis=1)
    kv_sets = [
        jnp.concatenate([own] + cp_fetch(free, own), axis=0)
        for own in (kv_own[t * rows : (t + 1) * rows] for t in range(trees))
    ]
    out_others = cp_fetch(free, tie(out_weight, query_low))
    out_full = jnp.concatenate([out_weight] + out_others, axis=1)
    clock = Clock()
    mixtures, lses, sums = [], [], []
    if shared:
        gate_line.step(query_low)
    for tree in range(trees):
        here = slice(tree * rows, (tree + 1) * rows)
        mixture, lse = clock.run(
            lambda q, kv, *_: attend(
                q, kv[:, :kv_width], kv[:, kv_width:], row_meta[tree], key_meta[tree], per_kv
            ),
            query_low[here],
            kv_sets[tree],
            cot_rows,
        )
        mixtures.append(mixture)
        lses.append(lse)
    gate_first = gate_line.got() if shared else ()
    for mixture in mixtures:
        sums.append(TpTotal(clock.run(lambda a, b, *_: matmul(a, b), mixture, out_full, *gate_first)))
    mixture_all = jnp.concatenate(mixtures, axis=0)
    if shared:
        gate_line.step()
    half_rows = up_weight.shape[0] // 2
    up_top = cp_fetch(free, tie(up_weight[:half_rows], *kv_sets, *out_others))
    for one in sums:
        one.across()
    gate_second = gate_line.got() if shared else ()
    sums[0].back(*gate_second)
    for one in sums[1:]:
        one.back(*gate_second, *up_top)
    if shared:
        gate_line.step()
    down_line = share_of(down_weight, *up_top)
    up_after = [down_line.right[0]] if shared else up_top
    up_bottom = cp_fetch(free, tie(up_weight[half_rows:], *up_after))
    up_others = [piece for pair in zip(up_top, up_bottom) for piece in pair]
    gate_others = [] if shared else cp_fetch(free, gate_weight)
    down_others = [] if shared else cp_fetch(free, down_weight)
    gate_full = clock.run(lambda w: assemble(w, gate_others, gate_line, False), gate_weight)
    hidden = input_wide + resid_scale * jnp.concatenate([one.value() for one in sums], axis=0).astype(wide)

    scale_ffn = lax.rsqrt(jnp.mean(hidden * hidden, axis=-1, keepdims=True) + norm_eps)
    unit_ffn = hidden * scale_ffn
    normed_ffn = (unit_ffn * ffn_gain_full).astype(low)
    gate_pre = clock.run(matmul, normed_ffn, gate_full)
    up_proj = clock.run(matmul, normed_ffn[:, :block], up_weight)
    for index, piece in enumerate(up_others):
        first = block + index * half_rows
        up_proj = up_proj + matmul(normed_ffn[:, first : first + half_rows], piece)
    up_full = jnp.concatenate([up_weight] + up_others, axis=0)
    activation = (gate_pre * jax.nn.sigmoid(gate_pre) * up_proj).astype(low)
    if shared:
        for _ in range(grp_count - 1):
            down_line.step()
    down_full = assemble(down_weight, down_others, down_line, True)

    sums_line = LineSum(clock)
    arrivals, keeps = [], []

    def blocks_of(values):
        return [values[:, s * block : (s + 1) * block] for s in range(cp_count)]

    def send(product, model_side, other_side):
        arrivals.append(
            [
                cp_deliver(
                    lane,
                    clock.run(lambda m, o: product(m, o).astype(low), model_side[s], other_side),
                    s,
                )
                for s in range(1, cp_count)
            ]
        )
        keeps.append((product, model_side[0], other_side))

    def arrive():
        index = sum(part is not None for part in sums_line.parts)
        product, model_side, other_side = keeps[index]

        def total(m, o, *got):
            whole = product(m, o)
            for piece in got:
                whole = whole + piece.astype(wide)
            return whole.astype(low)

        sums_line.load(clock.run(total, model_side, other_side, *arrivals[index]))

    model_last = lambda m, o: matmul_tn(o, m)
    model_first = matmul_tn
    upstream = cot_rows.astype(wide)
    down_in = (resid_scale * upstream).astype(low)
    down_in_blocks = blocks_of(down_in)
    hidden_units = activation.shape[1]
    quarter, half = hidden_units // 4, hidden_units // 2
    send(model_last, down_in_blocks, activation[:, : quarter // 2])
    send(model_last, down_in_blocks, activation[:, quarter // 2 : quarter])
    send(model_last, down_in_blocks, activation[:, quarter:half])

    def unit_grads(down_in, down_full, gate_pre, up_proj):
        hidden_grad = matmul_nt(down_in, down_full)
        gate_sig = jax.nn.sigmoid(gate_pre)
        gate_in = hidden_grad * up_proj * gate_sig * (1.0 + gate_pre * (1.0 - gate_sig))
        return gate_in.astype(low), (hidden_grad * gate_pre * gate_sig).astype(low)

    send(model_last, down_in_blocks, activation[:, half:])
    step = sums_line.step
    arrive()
    step()
    arrive()
    step()
    gate_in, upper_in = clock.run(unit_grads, down_in, down_full, gate_pre, up_proj)
    arrive()
    step()
    normed_ffn_blocks = blocks_of(normed_ffn)
    send(model_first, normed_ffn_blocks, gate_in[:, :half])
    arrive()
    step()
    ffn_part = clock.run(
        lambda a, b, c, d: matmul_nt(a, b) + matmul_nt(c, d), gate_in, gate_full, upper_in, up_full
    )
    send(model_first, normed_ffn_blocks, gate_in[:, half:])
    arrive()
    step()
    ffn_sum = TpTotal(tie(ffn_part, *clock.last))
    send(model_first, normed_ffn_blocks, upper_in[:, :half])
    ffn_sum.across(*clock.last)
    arrive()
    step()
    ffn_sum.back(*clock.last)
    send(model_first, normed_ffn_blocks, upper_in[:, half:])

    def hidden_grads(ffn_norm_grad, hidden, scale_ffn, upstream, ffn_gain_full):
        ffn_norm_grad = ffn_norm_grad.astype(wide)
        unit_ffn = hidden * scale_ffn
        hidden_back = upstream + norm_back(ffn_norm_grad, unit_ffn, scale_ffn, ffn_gain_full)
        return (
            (resid_scale * hidden_back).astype(low),
            hidden_back,
            jnp.sum(ffn_norm_grad * unit_ffn, axis=0),
        )

    attn_in, hidden_back, ffn_gain_part = clock.run(
        hidden_grads, ffn_sum.value(), hidden, scale_ffn, upstream, ffn_gain_full
    )
    attn_in_blocks = blocks_of(attn_in)
    mix_grad = clock.run(lambda a, b: matmul_nt(a, b).astype(low), attn_in, out_full)

    def attention_grads(tree):
        here = slice(tree * rows, (tree + 1) * rows)
        lse = lses[tree][:, ::HD].T.reshape(-1, 2, rows)
        dq, dk, dv = clock.run(
            lambda grad, q, kv, lse: attend_back(
                q,
                kv[:, :kv_width],
                kv[:, kv_width:],
                grad,
                lse,
                row_meta_t[tree],
                key_meta_t[tree],
                per_kv,
            ),
            mix_grad[here],
            query_low[here],
            kv_sets[tree],
            lse,
        )
        dkv = jnp.concatenate([dk, dv], axis=1)
        got = [
            cp_deliver(lane, dkv[s * rows : (s + 1) * rows].astype(low), s)
            for s in range(1, cp_count)
        ]
        return dq, dkv[:rows], got

    tree_grads = [attention_grads(0)]
    arrive()
    step()
    tree_grads += [attention_grads(tree) for tree in range(1, trees)]
    send(model_last, attn_in_blocks, mixture_all)
    arrive()
    step()

    def qkv_grads(cos_qk, sin_qk, *parts):
        queries, own, got = parts[:trees], parts[trees : 2 * trees], parts[2 * trees :]
        each = len(got) // trees
        sums = []
        for tree in range(trees):
            total = own[tree]
            for piece in got[tree * each : (tree + 1) * each]:
                total = total + piece.astype(wide)
            sums.append(total)
        kv_turned = jnp.concatenate(sums, axis=0)
        qk_turned = jnp.concatenate(
            [jnp.concatenate(queries, axis=0), kv_turned[:, :kv_width]], axis=1
        )
        qk_in = qk_turned * cos_qk - turn(qk_turned) * sin_qk
        return jnp.concatenate([qk_in, kv_turned[:, kv_width:]], axis=1).astype(low)

    qkv_in = clock.run(
        qkv_grads,
        cos_qk,
        sin_qk,
        *[g[0] for g in tree_grads],
        *[g[1] for g in tree_grads],
        *[piece for g in tree_grads for piece in g[2]],
    )
    normed_attn_blocks = blocks_of(normed_attn)
    send(model_last, normed_attn_blocks, qkv_in[:, :q_width])
    attn_part = clock.run(matmul_nt, qkv_in, qkv_full)
    arrive()
    step()
    attn_sum = TpTotal(tie(attn_part, *clock.last))
    send(model_last, normed_attn_blocks, qkv_in[:, q_width:])
    attn_sum.across(*clock.last)
    arrive()
    step()
    attn_sum.back(*clock.last)

    def input_grads(attn_norm_grad, input_wide, scale_attn, hidden_back, attn_gain_full):
        attn_norm_grad = attn_norm_grad.astype(wide)
        unit_attn = input_wide * scale_attn
        input_back = hidden_back + norm_back(attn_norm_grad, unit_attn, scale_attn, attn_gain_full)
        return width_part(input_back, tp_here), jnp.sum(attn_norm_grad * unit_attn, axis=0)

    arrive()
    step()
    input_mine, attn_gain_part = clock.run(
        input_grads, attn_sum.value(), input_wide, scale_attn, hidden_back, attn_gain_full
    )
    gain_rows = 16
    gain_part = jnp.concatenate(
        [attn_gain_part[None], ffn_gain_part[None], jnp.zeros((gain_rows - 2, model_width), wide)]
    )
    send(lambda m, o: m, blocks_of(gain_part), gain_part)
    arrive()
    step()
    down_mine = tp_scatter(clock.run(matmul, activation, down_full))
    result = (width_part(hidden, tp_here) + resid_scale * down_mine).astype(low)
    for _ in range(LineSum.lag):
        sums_line.load(None)
        step()
    finals = [sums_line.final(index) for index in range(len(keeps))]
    down_grad = jnp.concatenate(finals[0:4], axis=0)
    gate_grad = jnp.concatenate(finals[4:6], axis=1)
    up_grad = jnp.concatenate(finals[6:8], axis=1)
    out_grad, query_grad, kv_grad, gain_grads = finals[8], finals[9].T, finals[10].T, finals[11]
    return (
        result.reshape(inputs.shape),
        input_mine.reshape(inputs.shape),
        gain_grads[0],
        query_grad,
        kv_grad[:, :kv_width],
        kv_grad[:, kv_width:],
        out_grad,
        gain_grads[1],
        gate_grad,
        up_grad,
        down_grad,
    )


def solution(mesh):
    in_specs = (
        P("grp", "cp", "tp"),
        P("grp", "cp", "tp"),
        P("cp"),
        P("cp", "tp"),
        P("cp", "tp"),
        P("cp", "tp"),
        P("tp", "cp"),
        P("cp"),
        P("cp", "tp"),
        P("cp", "tp"),
        P("tp", "cp"),
        P("grp", None),
        P("grp", None),
        P("grp", None),
        P("grp", None),
    )
    out_specs = (
        P("grp", "cp", "tp"),
        P("grp", "cp", "tp"),
        P("cp"),
        P("cp", "tp"),
        P("cp", "tp"),
        P("cp", "tp"),
        P("tp", "cp"),
        P("cp"),
        P("cp", "tp"),
        P("cp", "tp"),
        P("tp", "cp"),
    )
    return jax.shard_map(
        per_device, mesh=mesh, in_specs=in_specs, out_specs=out_specs, check_vma=False
    )
```

```python
import functools
import math

import jax
import jax.numpy as jnp
from jax import lax
from jax.experimental import pallas as pl
from jax.experimental.pallas import tpu as pltpu
from jax.sharding import PartitionSpec as P

HD = 64

norm_eps = 1e-05
att_scale = 0.015625
resid_scale = 0.22
rope_base = 10000000.0
masked_score = -1e30

low = jnp.bfloat16
wide = jnp.float32


def tie(value, *earlier):
    return lax.optimization_barrier((value,) + earlier)[0] if earlier else value


class Lane:
    def __init__(self, depth):
        self.depth = depth
        self.done = []

    def move(self, block, axis, pairs, *earlier):
        if len(self.done) >= self.depth:
            earlier = (self.done[-self.depth],) + earlier
        self.done.append(lax.ppermute(tie(block, *earlier), axis, pairs))
        return self.done[-1]


class Clock:
    def __init__(self):
        self.last = ()

    def run(self, function, *given):
        given = lax.optimization_barrier(given + self.last)[: len(given)]
        result = function(*given)
        self.last = (jax.tree.leaves(result)[0],)
        return result


def cp_fetch(lane, block):
    count = lax.axis_size("cp")
    return [
        lane.move(block, "cp", [((i + s) % count, i) for i in range(count)])
        for s in range(1, count)
    ]


def cp_deliver(lane, block, shift):
    count = lax.axis_size("cp")
    return lane.move(block, "cp", [(i, (i + shift) % count) for i in range(count)])


def in_order(flag, first, second):
    return [jnp.where(flag, first, second), jnp.where(flag, second, first)]


class LineGather:
    def __init__(self, block):
        self.right, self.left = [block], [block]

    def step(self, *earlier):
        last = lax.axis_size("grp") - 1
        self.right.append(
            lax.ppermute(tie(self.right[-1], *earlier), "grp", [(i, i + 1) for i in range(last)])
        )
        self.left.append(
            lax.ppermute(tie(self.left[-1], *earlier), "grp", [(i + 1, i) for i in range(last)])
        )

    def got(self):
        return self.right[-1], self.left[-1]


def assemble_kernel(here_ref, own_ref, *refs, own_blocks, share_blocks, beside):
    step, here = pl.program_id(0), here_ref[0]
    share_ref, *moved_refs, out_ref = refs
    width = own_ref.shape[1]
    place = step if beside else step - own_blocks
    target = out_ref.at[:, width:] if beside else out_ref
    if beside:
        out_ref[:, :width] = own_ref[...]
    else:

        @pl.when(place < 0)
        def _():
            target[...] = own_ref[...]

    owner = lax.div(jnp.maximum(place, 0), share_blocks)
    away = len(moved_refs) // 2
    for shift, ref in zip([0, *range(1, away + 1), *range(-1, -away - 1, -1)], [share_ref, *moved_refs]):

        @pl.when((place >= 0) & (owner == here - shift))
        def _():
            target[...] = ref[...]


def assemble_shared(weight, line, beside):
    share = line.right[0].shape[0]
    rows, width = weight.shape
    unit = math.gcd(rows, share)
    own_blocks, share_blocks = rows // unit, share // unit
    offset = 0 if beside else own_blocks
    spec = lambda first, count: pl.BlockSpec(
        (unit, width), lambda i, here: (jnp.clip(i - first(here[0]), 0, count - 1), 0)
    )
    moved = lambda shift: spec(lambda z: offset + (z - shift) * share_blocks, share_blocks)
    away = len(line.right) - 1
    specs = [spec(lambda z: 0, own_blocks)]
    specs += [moved(shift) for shift in [*range(away + 1), *range(-1, -away - 1, -1)]]
    out_shape = (rows, 2 * width) if beside else (2 * rows, width)
    return pl.pallas_call(
        functools.partial(
            assemble_kernel, own_blocks=own_blocks, share_blocks=share_blocks, beside=beside
        ),
        grid_spec=pltpu.PrefetchScalarGridSpec(
            num_scalar_prefetch=1,
            grid=(out_shape[0] // unit,),
            in_specs=specs,
            out_specs=pl.BlockSpec((unit, out_shape[1]), lambda i, here: (i, 0)),
        ),
        out_shape=jax.ShapeDtypeStruct(out_shape, weight.dtype),
        cost_estimate=pl.CostEstimate(
            flops=0, bytes_accessed=8 * rows * width + 2 * share * width, transcendentals=0
        ),
        name="assemble",
    )(
        lax.axis_index("grp").astype(jnp.int32).reshape(1),
        weight,
        *line.right,
        *line.left[1:],
    )


class LineSum:
    lag = 3

    def __init__(self, clock):
        here = lax.axis_index("grp")
        self.inner = (here == 1) | (here == 2)
        self.clock = clock
        self.parts, self.sums, self.totals = [], [], []
        self.ins, self.acrosses, self.outs, self.loads = [], [], [], []

    def load(self, part):
        self.parts.append(part)
        back = len(self.parts) - 1 - self.lag
        total = self.totals[back] if back >= 0 else None
        if part is None or total is None or part.shape[1] != total.shape[1]:
            self.loads.append((part, total))
            return
        height = max(part.shape[0], total.shape[0])

        def choose(part, total):
            fill = lambda v: jnp.pad(v, ((0, height - v.shape[0]), (0, 0)))
            return jnp.where(self.inner, fill(total), fill(part))

        self.loads.append(self.clock.run(choose, part, total))

    def step(self):
        count = len(self.loads) - 1
        before = self.ins[-2:-1] + self.outs[-2:-1]
        load = self.loads[count]
        if isinstance(load, tuple):
            part, total = load
            if part is not None:
                self.ins.append(lax.ppermute(tie(part, *before), "grp", [(0, 1), (3, 2)]))
            if total is not None:
                self.outs.append(lax.ppermute(tie(total, *before), "grp", [(1, 0), (2, 3)]))
        else:
            side = lax.ppermute(tie(load, *before), "grp", [(0, 1), (1, 0), (2, 3), (3, 2)])
            self.ins.append(side)
            self.outs.append(side)
        if count >= 1 and self.parts[count - 1] is not None:
            part, got = self.parts[count - 1], self.ins[count - 1]
            total = self.clock.run(lambda p, g: p + g[: p.shape[0]], part, got)
            self.sums.append(total)
            self.acrosses.append(
                lax.ppermute(tie(total, *self.acrosses[-1:]), "grp", [(1, 2), (2, 1)])
            )
        if count >= 2 and self.parts[count - 2] is not None:
            self.totals.append(
                self.clock.run(lambda a, b: a + b, self.sums[count - 2], self.acrosses[count - 2])
            )

    def final(self, index):
        total, got = self.totals[index], self.outs[index]
        return jnp.where(self.inner, total, got[: total.shape[0]]).astype(wide)


def tp_swap(block, bit, *earlier):
    count = lax.axis_size("tp")
    return lax.ppermute(tie(block, *earlier), "tp", [(i, i ^ bit) for i in range(count)])


class TpTotal:
    def __init__(self, part):
        self.plain = None
        if lax.axis_size("tp") != 4:
            self.plain = lax.psum(part.astype(low), "tp")
            return
        half = part.shape[0] // 2
        self.odd = lax.axis_index("tp") % 2
        self.mine = lax.dynamic_slice_in_dim(part, self.odd * half, half, 0)
        theirs = lax.dynamic_slice_in_dim(part, (1 - self.odd) * half, half, 0)
        self.got = tp_swap(theirs.astype(low), 1)

    def across(self, *earlier):
        if self.plain is None:
            self.pair = (self.mine.astype(wide) + self.got.astype(wide)).astype(low)
            self.far = tp_swap(self.pair, 2, *earlier)
            return self.far
        return self.plain

    def back(self, *earlier):
        if self.plain is None:
            self.total = (self.pair.astype(wide) + self.far.astype(wide)).astype(low)
            self.other = tp_swap(self.total, 1, *earlier)
            return self.other
        return self.plain

    def value(self):
        if self.plain is None:
            return jnp.concatenate(in_order(self.odd == 0, self.total, self.other), axis=0)
        return self.plain


def attend_kernel(
    q_ref, k_ref, v_ref, row_ref, col_ref, o_ref, lse_ref, bias_ref, *, per_kv
):
    step = pl.program_id(0)
    group = (2 * step) // per_kv

    @pl.when(step == 0)
    def _():
        seg, par, grand, pos = (row_ref[:, i : i + 1] for i in range(4))
        key_seg, key_pos = col_ref[0:1, :], col_ref[1:2, :]
        linked = (key_seg == seg) | (key_seg == par) | (key_seg == grand)
        bias_ref[...] = jnp.where(linked & (key_pos <= pos), 0.0, masked_score)

    k = jnp.where(group == 0, k_ref[:, :HD], k_ref[:, HD : 2 * HD])
    v = jnp.where(group == 0, v_ref[:, :HD], v_ref[:, HD : 2 * HD])
    outs, totals = [], []
    for h in range(2):
        q = q_ref[:, h * HD : (h + 1) * HD]
        s = lax.dot_general(q, k, (((1,), (1,)), ((), ())), preferred_element_type=wide)
        s = s + bias_ref[...]
        top = jnp.max(s, axis=-1, keepdims=True)
        p = jnp.exp(s - top)
        norm = jnp.sum(p, axis=-1, keepdims=True)
        o = jnp.dot(p.astype(low), v, preferred_element_type=wide)
        outs.append(o / norm)
        totals.append(top + jnp.log(norm))
    o_ref[...] = jnp.concatenate(outs, axis=1).astype(low)
    lse_ref[...] = jnp.concatenate([jnp.broadcast_to(t, (t.shape[0], HD)) for t in totals], axis=1)


def attend(q, k, v, row_meta, col_meta, per_kv):
    rows, width = q.shape
    keys, kv_width = k.shape
    pairs = width // (2 * HD)
    whole = lambda a: pl.BlockSpec(a.shape, lambda j: (0, 0))
    tile = pl.BlockSpec((rows, 2 * HD), lambda j: (0, j))
    heads = 2 * pairs
    return pl.pallas_call(
        functools.partial(attend_kernel, per_kv=per_kv),
        grid=(pairs,),
        in_specs=[tile, whole(k), whole(v), whole(row_meta), whole(col_meta)],
        out_specs=[tile, tile],
        out_shape=[
            jax.ShapeDtypeStruct((rows, width), low),
            jax.ShapeDtypeStruct((rows, width), wide),
        ],
        scratch_shapes=[pltpu.VMEM((rows, keys), wide)],
        cost_estimate=pl.CostEstimate(
            flops=16 * heads * rows * keys * HD,
            bytes_accessed=8 * rows * width + 4 * keys * kv_width,
            transcendentals=heads * rows * keys,
        ),
        name="attend",
    )(q, k, v, row_meta, col_meta)


def attend_back_kernel(
    q_ref, k_ref, v_ref, g_ref, lse_ref, row_ref, col_ref, dq_ref, dk_ref, dv_ref, bias_ref, dk_sum, dv_sum, *, per_kv
):
    step = pl.program_id(0)
    group = (2 * step) // per_kv
    pairs_kv = per_kv // 2

    @pl.when(step == 0)
    def _():
        seg, par, grand, pos = (row_ref[i : i + 1, :] for i in range(4))
        key_seg, key_pos = col_ref[:, 0:1], col_ref[:, 1:2]
        linked = (key_seg == seg) | (key_seg == par) | (key_seg == grand)
        bias_ref[...] = jnp.where(linked & (key_pos <= pos), 0.0, masked_score)

    k = jnp.where(group == 0, k_ref[:, :HD], k_ref[:, HD : 2 * HD])
    v = jnp.where(group == 0, v_ref[:, :HD], v_ref[:, HD : 2 * HD])
    outs = []
    dk = jnp.zeros(k.shape, wide)
    dv = jnp.zeros(k.shape, wide)
    nt = (((1,), (1,)), ((), ()))
    for h in range(2):
        q = q_ref[:, h * HD : (h + 1) * HD]
        g = g_ref[:, h * HD : (h + 1) * HD]
        s = lax.dot_general(k, q, nt, preferred_element_type=wide) + bias_ref[...]
        p = jnp.exp(s - lse_ref[0, h : h + 1, :])
        dp = lax.dot_general(v, g, nt, preferred_element_type=wide)
        dv = dv + jnp.dot(p.astype(low), g, preferred_element_type=wide)
        mean = jnp.sum(p * dp, axis=0, keepdims=True)
        dz = (p * (dp - mean)).astype(low)
        dk = dk + jnp.dot(dz, q, preferred_element_type=wide)
        dq = lax.dot_general(dz, k, (((0,), (0,)), ((), ())), preferred_element_type=wide)
        outs.append(dq * att_scale)
    dq_ref[...] = jnp.concatenate(outs, axis=1)
    first = lax.rem(step, pairs_kv) == 0

    @pl.when(first)
    def _():
        dk_sum[...] = dk
        dv_sum[...] = dv

    @pl.when(jnp.logical_not(first))
    def _():
        dk_sum[...] += dk
        dv_sum[...] += dv

    for which in range(2):

        @pl.when(step == (which + 1) * pairs_kv - 1)
        def _():
            dk_ref[:, which * HD : (which + 1) * HD] = dk_sum[...]
            dv_ref[:, which * HD : (which + 1) * HD] = dv_sum[...]


def attend_back(q, k, v, g, lse, row_meta, col_meta, per_kv):
    rows, width = q.shape
    keys, kv_width = k.shape
    pairs = width // (2 * HD)
    heads = 2 * pairs
    whole = lambda a: pl.BlockSpec(a.shape, lambda j: (0, 0))
    tile = pl.BlockSpec((rows, 2 * HD), lambda j: (0, j))
    return pl.pallas_call(
        functools.partial(attend_back_kernel, per_kv=per_kv),
        grid=(pairs,),
        in_specs=[
            tile,
            whole(k),
            whole(v),
            tile,
            pl.BlockSpec((1, 2, rows), lambda j: (j, 0, 0)),
            whole(row_meta),
            whole(col_meta),
        ],
        out_specs=[tile, whole(k), whole(v)],
        out_shape=[
            jax.ShapeDtypeStruct((rows, width), wide),
            jax.ShapeDtypeStruct((keys, kv_width), wide),
            jax.ShapeDtypeStruct((keys, kv_width), wide),
        ],
        scratch_shapes=[
            pltpu.VMEM((keys, rows), wide),
            pltpu.VMEM((keys, HD), wide),
            pltpu.VMEM((keys, HD), wide),
        ],
        cost_estimate=pl.CostEstimate(
            flops=40 * heads * rows * keys * HD,
            bytes_accessed=8 * rows * width + 12 * keys * kv_width,
            transcendentals=heads * rows * keys,
        ),
        name="attend_back",
    )(q, k, v, g, lse, row_meta, col_meta)


def rope_tables(position, repeats):
    half_dim = HD // 2
    freq_index = jnp.arange(half_dim, dtype=wide)
    inverse = jnp.power(wide(rope_base), freq_index * (-2.0 / HD))
    angles = position.astype(wide)[:, None] * inverse
    tile = lambda table: jnp.tile(table, (1, 2 * repeats))
    return tile(jnp.cos(angles)), tile(jnp.sin(angles))


def turn(values):
    half_dim = HD // 2
    front = lax.broadcasted_iota(jnp.int32, values.shape, 1) % HD < half_dim
    return jnp.where(
        front, -jnp.roll(values, -half_dim, axis=1), jnp.roll(values, half_dim, axis=1)
    )


def norm_back(norm_grad, normed_unit, inv_scale, gain_vec):
    scaled = norm_grad * gain_vec
    return inv_scale * (
        scaled - normed_unit * jnp.mean(scaled * normed_unit, axis=-1, keepdims=True)
    )


def matmul(a, b):
    return jnp.dot(a, b, preferred_element_type=wide)


def matmul_nt(a, b):
    return lax.dot_general(a, b, (((1,), (1,)), ((), ())), preferred_element_type=wide)


def matmul_tn(a, b):
    return lax.dot_general(a, b, (((0,), (0,)), ((), ())), preferred_element_type=wide)


def tree_segments(seg_parent, seg_start, seg_len, key_count):
    token_ids = jnp.arange(key_count, dtype=jnp.int32)
    slot_ids = jnp.arange(seg_parent.shape[1], dtype=jnp.int32)
    member = (token_ids[None, :, None] >= seg_start[:, None, :]) & (
        token_ids[None, :, None] < (seg_start + seg_len)[:, None, :]
    )
    pick = lambda table: jnp.sum(jnp.where(member, table[:, None, :], 0), axis=2)
    grand_parent = jnp.sum(
        jnp.where(seg_parent[:, :, None] == slot_ids[None, None, :], seg_parent[:, None, :], 0),
        axis=2,
    )
    return (
        pick(jnp.broadcast_to(slot_ids[None, :], seg_parent.shape)),
        pick(seg_parent),
        pick(grand_parent),
    )


def per_device(
    inputs,
    cotangent,
    attn_gain,
    query_weight,
    key_weight,
    value_weight,
    out_weight,
    ffn_gain,
    gate_weight,
    up_weight,
    down_weight,
    seg_parent,
    seg_start,
    seg_len,
    positions,
):
    trees, rows, part_width = inputs.shape
    keys = positions.shape[1]
    block = attn_gain.shape[0]
    cp_count, tp_count, grp_count = lax.axis_size("cp"), lax.axis_size("tp"), lax.axis_size("grp")
    model_width = block * cp_count
    q_width, kv_width = query_weight.shape[1], key_weight.shape[1]
    per_kv = q_width // kv_width
    tokens = trees * rows
    cp_here, tp_here = lax.axis_index("cp"), lax.axis_index("tp")

    def rolled(values):
        return lax.dynamic_slice_in_dim(
            jnp.concatenate([values, values], axis=-1), cp_here * block, model_width, values.ndim - 1
        )

    def width_part(values, owner):
        start = (owner * part_width - cp_here * block) % model_width
        if block % part_width:
            values = jnp.concatenate([values, values], axis=-1)
        return lax.dynamic_slice_in_dim(values, start, part_width, 1)

    def tp_width(shard, *earlier):
        shard = tie(shard.reshape(tokens, part_width), *earlier)
        if tp_count != 4:
            return rolled(lax.all_gather(shard, "tp", axis=1, tiled=True)), shard
        far = tp_swap(shard, 2)
        near = tp_swap(jnp.stack([shard, far]), 1)
        pieces = [shard, near[0], far, near[1]]
        picks = [lax.select_n(tp_here, *[pieces[j ^ m] for m in range(4)]) for j in range(4)]
        return rolled(jnp.concatenate(picks, axis=1)), far

    def tp_scatter(part):
        if tp_count != 4:
            natural = lax.dynamic_slice_in_dim(
                jnp.concatenate([part, part], axis=-1),
                (model_width - cp_here * block) % model_width,
                model_width,
                1,
            )
            return lax.psum_scatter(
                natural.astype(low), "tp", scatter_dimension=1, tiled=True
            ).astype(wide)
        sent = jnp.concatenate([width_part(part, tp_here ^ 1), width_part(part, tp_here ^ 3)], axis=1)
        got = tp_swap(sent.astype(low), 1).astype(wide)
        kept = width_part(part, tp_here) + got[:, :part_width]
        passed = width_part(part, tp_here ^ 2) + got[:, part_width:]
        return kept + tp_swap(passed.astype(low), 2).astype(wide)

    free, lane = Lane(64), Lane(2)
    shared = cp_count == 2 and grp_count == 4

    def share_of(weight, *earlier):
        if not shared:
            return None
        share = weight.shape[0] // grp_count
        part = lax.dynamic_slice_in_dim(weight, lax.axis_index("grp") * share, share, 0)
        return LineGather(cp_fetch(free, tie(part, *earlier))[0])

    def assemble(weight, others, gathered, beside):
        if shared:
            return assemble_shared(weight, gathered, beside)
        return jnp.concatenate([weight] + others, axis=1 if beside else 0)

    qkv_own = jnp.concatenate([query_weight, key_weight, value_weight], axis=1)
    gains_own = jnp.stack([attn_gain, ffn_gain])
    qkv_others = cp_fetch(free, qkv_own)
    gains = jnp.concatenate([gains_own] + cp_fetch(free, gains_own), axis=1).astype(wide)
    attn_gain_full, ffn_gain_full = gains[0:1], gains[1:2]
    qkv_full = jnp.concatenate([qkv_own] + qkv_others, axis=0)
    input_rows, input_far = tp_width(inputs)
    input_rows = tie(input_rows, *qkv_others)
    gate_line = share_of(gate_weight)
    cot_rows, _ = tp_width(cotangent, input_far)

    seg, parent, grand = tree_segments(seg_parent, seg_start, seg_len, keys)
    meta = jnp.stack([seg, parent, grand, positions], axis=1)
    first_row = cp_here * rows
    row_meta_t = lax.dynamic_slice_in_dim(meta, first_row, rows, 2)
    key_meta = lax.dynamic_slice_in_dim(
        jnp.concatenate([meta[:, 0::3], meta[:, 0::3]], axis=2), first_row, keys, 2
    )
    row_meta = jnp.swapaxes(row_meta_t, 1, 2)
    key_meta_t = jnp.swapaxes(key_meta, 1, 2)
    own_pos = row_meta_t[:, 3].reshape(tokens)
    cos_qk, sin_qk = rope_tables(own_pos, (q_width + kv_width) // HD)

    input_wide = input_rows.astype(wide)
    scale_attn = lax.rsqrt(jnp.mean(input_wide * input_wide, axis=-1, keepdims=True) + norm_eps)
    unit_attn = input_wide * scale_attn
    normed_attn = (unit_attn * attn_gain_full).astype(low)
    qkv_raw = matmul(normed_attn, qkv_full)
    qk_raw = qkv_raw[:, : q_width + kv_width]
    qk_rot = qk_raw * cos_qk + turn(qk_raw) * sin_qk
    query_low = qk_rot[:, :q_width].astype(low) * low(att_scale)
    key_low = qk_rot[:, q_width:].astype(low)
    kv_own = jnp.concatenate([key_low, qkv_raw[:, q_width + kv_width :].astype(low)], axis=1)
    kv_sets = [
        jnp.concatenate([own] + cp_fetch(free, own), axis=0)
        for own in (kv_own[t * rows : (t + 1) * rows] for t in range(trees))
    ]
    out_others = cp_fetch(free, tie(out_weight, query_low))
    out_full = jnp.concatenate([out_weight] + out_others, axis=1)
    clock = Clock()
    mixtures, lses, sums = [], [], []
    if shared:
        gate_line.step(query_low)
    for tree in range(trees):
        here = slice(tree * rows, (tree + 1) * rows)
        mixture, lse = clock.run(
            lambda q, kv, *_: attend(
                q, kv[:, :kv_width], kv[:, kv_width:], row_meta[tree], key_meta[tree], per_kv
            ),
            query_low[here],
            kv_sets[tree],
            cot_rows,
        )
        mixtures.append(mixture)
        lses.append(lse)
    gate_first = gate_line.got() if shared else ()
    for mixture in mixtures:
        sums.append(TpTotal(clock.run(lambda a, b, *_: matmul(a, b), mixture, out_full, *gate_first)))
    mixture_all = jnp.concatenate(mixtures, axis=0)
    if shared:
        gate_line.step()
    half_rows = up_weight.shape[0] // 2
    up_top = cp_fetch(free, tie(up_weight[:half_rows], *kv_sets, *out_others))
    for one in sums:
        one.across()
    gate_second = gate_line.got() if shared else ()
    sums[0].back(*gate_second)
    for one in sums[1:]:
        one.back(*gate_second, *up_top)
    if shared:
        gate_line.step()
    down_line = share_of(down_weight, *up_top)
    up_after = [down_line.right[0]] if shared else up_top
    up_bottom = cp_fetch(free, tie(up_weight[half_rows:], *up_after))
    up_others = [piece for pair in zip(up_top, up_bottom) for piece in pair]
    gate_others = [] if shared else cp_fetch(free, gate_weight)
    down_others = [] if shared else cp_fetch(free, down_weight)
    gate_full = clock.run(lambda w: assemble(w, gate_others, gate_line, False), gate_weight)
    hidden = input_wide + resid_scale * jnp.concatenate([one.value() for one in sums], axis=0).astype(wide)

    scale_ffn = lax.rsqrt(jnp.mean(hidden * hidden, axis=-1, keepdims=True) + norm_eps)
    unit_ffn = hidden * scale_ffn
    normed_ffn = (unit_ffn * ffn_gain_full).astype(low)
    gate_pre = clock.run(matmul, normed_ffn, gate_full)
    up_proj = clock.run(matmul, normed_ffn[:, :block], up_weight)
    for index, piece in enumerate(up_others):
        first = block + index * half_rows
        up_proj = up_proj + matmul(normed_ffn[:, first : first + half_rows], piece)
    up_full = jnp.concatenate([up_weight] + up_others, axis=0)
    activation = (gate_pre * jax.nn.sigmoid(gate_pre) * up_proj).astype(low)
    if shared:
        for _ in range(grp_count - 1):
            down_line.step()
    down_full = assemble(down_weight, down_others, down_line, True)

    sums_line = LineSum(clock)
    arrivals, keeps = [], []

    def blocks_of(values):
        return [values[:, s * block : (s + 1) * block] for s in range(cp_count)]

    def send(product, model_side, other_side):
        arrivals.append(
            [
                cp_deliver(
                    lane,
                    clock.run(lambda m, o: product(m, o).astype(low), model_side[s], other_side),
                    s,
                )
                for s in range(1, cp_count)
            ]
        )
        keeps.append((product, model_side[0], other_side))

    def arrive():
        index = sum(part is not None for part in sums_line.parts)
        product, model_side, other_side = keeps[index]

        def total(m, o, *got):
            whole = product(m, o)
            for piece in got:
                whole = whole + piece.astype(wide)
            return whole.astype(low)

        sums_line.load(clock.run(total, model_side, other_side, *arrivals[index]))

    model_last = lambda m, o: matmul_tn(o, m)
    model_first = matmul_tn
    upstream = cot_rows.astype(wide)
    down_in = (resid_scale * upstream).astype(low)
    down_in_blocks = blocks_of(down_in)
    hidden_units = activation.shape[1]
    quarter, half = hidden_units // 4, hidden_units // 2
    send(model_last, down_in_blocks, activation[:, : quarter // 2])
    send(model_last, down_in_blocks, activation[:, quarter // 2 : quarter])
    send(model_last, down_in_blocks, activation[:, quarter:half])

    def unit_grads(down_in, down_full, gate_pre, up_proj):
        hidden_grad = matmul_nt(down_in, down_full)
        gate_sig = jax.nn.sigmoid(gate_pre)
        gate_in = hidden_grad * up_proj * gate_sig * (1.0 + gate_pre * (1.0 - gate_sig))
        return gate_in.astype(low), (hidden_grad * gate_pre * gate_sig).astype(low)

    send(model_last, down_in_blocks, activation[:, half:])
    step = sums_line.step
    arrive()
    step()
    arrive()
    step()
    gate_in, upper_in = clock.run(unit_grads, down_in, down_full, gate_pre, up_proj)
    arrive()
    step()
    normed_ffn_blocks = blocks_of(normed_ffn)
    send(model_first, normed_ffn_blocks, gate_in[:, :half])
    arrive()
    step()
    ffn_part = clock.run(
        lambda a, b, c, d: matmul_nt(a, b) + matmul_nt(c, d), gate_in, gate_full, upper_in, up_full
    )
    send(model_first, normed_ffn_blocks, gate_in[:, half:])
    arrive()
    step()
    ffn_sum = TpTotal(tie(ffn_part, *clock.last))
    send(model_first, normed_ffn_blocks, upper_in[:, :half])
    ffn_sum.across(*clock.last)
    arrive()
    step()
    ffn_sum.back(*clock.last)
    send(model_first, normed_ffn_blocks, upper_in[:, half:])

    def hidden_grads(ffn_norm_grad, hidden, scale_ffn, upstream, ffn_gain_full):
        ffn_norm_grad = ffn_norm_grad.astype(wide)
        unit_ffn = hidden * scale_ffn
        hidden_back = upstream + norm_back(ffn_norm_grad, unit_ffn, scale_ffn, ffn_gain_full)
        return (
            (resid_scale * hidden_back).astype(low),
            hidden_back,
            jnp.sum(ffn_norm_grad * unit_ffn, axis=0),
        )

    attn_in, hidden_back, ffn_gain_part = clock.run(
        hidden_grads, ffn_sum.value(), hidden, scale_ffn, upstream, ffn_gain_full
    )
    attn_in_blocks = blocks_of(attn_in)
    mix_grad = clock.run(lambda a, b: matmul_nt(a, b).astype(low), attn_in, out_full)

    def attention_grads(tree):
        here = slice(tree * rows, (tree + 1) * rows)
        lse = lses[tree][:, ::HD].T.reshape(-1, 2, rows)
        dq, dk, dv = clock.run(
            lambda grad, q, kv, lse: attend_back(
                q,
                kv[:, :kv_width],
                kv[:, kv_width:],
                grad,
                lse,
                row_meta_t[tree],
                key_meta_t[tree],
                per_kv,
            ),
            mix_grad[here],
            query_low[here],
            kv_sets[tree],
            lse,
        )
        dkv = jnp.concatenate([dk, dv], axis=1)
        got = [
            cp_deliver(lane, dkv[s * rows : (s + 1) * rows].astype(low), s)
            for s in range(1, cp_count)
        ]
        return dq, dkv[:rows], got

    tree_grads = [attention_grads(0)]
    arrive()
    step()
    tree_grads += [attention_grads(tree) for tree in range(1, trees)]
    send(model_last, attn_in_blocks, mixture_all)
    arrive()
    step()

    def qkv_grads(cos_qk, sin_qk, *parts):
        queries, own, got = parts[:trees], parts[trees : 2 * trees], parts[2 * trees :]
        each = len(got) // trees
        sums = []
        for tree in range(trees):
            total = own[tree]
            for piece in got[tree * each : (tree + 1) * each]:
                total = total + piece.astype(wide)
            sums.append(total)
        kv_turned = jnp.concatenate(sums, axis=0)
        qk_turned = jnp.concatenate(
            [jnp.concatenate(queries, axis=0), kv_turned[:, :kv_width]], axis=1
        )
        qk_in = qk_turned * cos_qk - turn(qk_turned) * sin_qk
        return jnp.concatenate([qk_in, kv_turned[:, kv_width:]], axis=1).astype(low)

    qkv_in = clock.run(
        qkv_grads,
        cos_qk,
        sin_qk,
        *[g[0] for g in tree_grads],
        *[g[1] for g in tree_grads],
        *[piece for g in tree_grads for piece in g[2]],
    )
    normed_attn_blocks = blocks_of(normed_attn)
    send(model_last, normed_attn_blocks, qkv_in[:, :q_width])
    attn_part = clock.run(matmul_nt, qkv_in, qkv_full)
    arrive()
    step()
    attn_sum = TpTotal(tie(attn_part, *clock.last))
    send(model_last, normed_attn_blocks, qkv_in[:, q_width:])
    attn_sum.across(*clock.last)
    arrive()
    step()
    attn_sum.back(*clock.last)

    def input_grads(attn_norm_grad, input_wide, scale_attn, hidden_back, attn_gain_full):
        attn_norm_grad = attn_norm_grad.astype(wide)
        unit_attn = input_wide * scale_attn
        input_back = hidden_back + norm_back(attn_norm_grad, unit_attn, scale_attn, attn_gain_full)
        return width_part(input_back, tp_here), jnp.sum(attn_norm_grad * unit_attn, axis=0)

    arrive()
    step()
    input_mine, attn_gain_part = clock.run(
        input_grads, attn_sum.value(), input_wide, scale_attn, hidden_back, attn_gain_full
    )
    gain_rows = 16
    gain_part = jnp.concatenate(
        [attn_gain_part[None], ffn_gain_part[None], jnp.zeros((gain_rows - 2, model_width), wide)]
    )
    send(lambda m, o: m, blocks_of(gain_part), gain_part)
    arrive()
    step()
    down_mine = tp_scatter(clock.run(matmul, activation, down_full))
    result = (width_part(hidden, tp_here) + resid_scale * down_mine).astype(low)
    for _ in range(LineSum.lag):
        sums_line.load(None)
        step()
    finals = [sums_line.final(index) for index in range(len(keeps))]
    down_grad = jnp.concatenate(finals[0:4], axis=0)
    gate_grad = jnp.concatenate(finals[4:6], axis=1)
    up_grad = jnp.concatenate(finals[6:8], axis=1)
    out_grad, query_grad, kv_grad, gain_grads = finals[8], finals[9].T, finals[10].T, finals[11]
    return (
        result.reshape(inputs.shape),
        input_mine.reshape(inputs.shape),
        gain_grads[0],
        query_grad,
        kv_grad[:, :kv_width],
        kv_grad[:, kv_width:],
        out_grad,
        gain_grads[1],
        gate_grad,
        up_grad,
        down_grad,
    )


def solution(mesh):
    in_specs = (
        P("grp", "cp", "tp"),
        P("grp", "cp", "tp"),
        P("cp"),
        P("cp", "tp"),
        P("cp", "tp"),
        P("cp", "tp"),
        P("tp", "cp"),
        P("cp"),
        P("cp", "tp"),
        P("cp", "tp"),
        P("tp", "cp"),
        P("grp", None),
        P("grp", None),
        P("grp", None),
        P("grp", None),
    )
    out_specs = (
        P("grp", "cp", "tp"),
        P("grp", "cp", "tp"),
        P("cp"),
        P("cp", "tp"),
        P("cp", "tp"),
        P("cp", "tp"),
        P("tp", "cp"),
        P("cp"),
        P("cp", "tp"),
        P("cp", "tp"),
        P("tp", "cp"),
    )
    return jax.shard_map(
        per_device, mesh=mesh, in_specs=in_specs, out_specs=out_specs, check_vma=False
    )
```
